32 devices in a mesh: groups: 2 (over y), expert: 4 (over z), dp: 4 (over x, core).
Axes of the slice: x: 2, y: 2, z: 4, core: 2. Of those that a mesh axis runs over, the one named last changes fastest.
Arguments:
- tokens: bfloat16 [2048, 1024], P(('groups', 'expert', 'dp')), parts along dimension 0, may hold values from -6 to 6
- expert_ids: int32 [2048, 8], P(('groups', 'expert', 'dp')), parts along dimension 0, may hold values from 0 to 31, all different within a row; in each aligned block of 64 rows (0 to 63, 64 to 127, ...) at most 32 rows name the same one
- route_scores: float32 [2048, 8], P(('groups', 'expert', 'dp')), parts along dimension 0, may hold values from 0.05 to 1
- w_gate: bfloat16 [32, 1024, 768], P('expert'), may hold values from -0.1875 to 0.1875
- w_up: bfloat16 [32, 1024, 768], P('expert'), may hold values from -0.1875 to 0.1875
- w_down: bfloat16 [32, 768, 1024], P('expert'), may hold values from -0.21875 to 0.21875
Outputs:
- mixed: bfloat16 [2048, 1024], P(('groups', 'expert', 'dp')), parts along dimension 0
The draws below stay inside these ranges and needn't reach their ends.
There are 2 independent parts, one for each index of `groups`. The reference program is written for one: setup_inputs(seed, part) draws one part's arguments, and reference() takes and returns one part's arrays. A program takes and returns all parts, laid end to end along the dimension named above; an argument that names none is the same for every part. Nothing has to cross between parts.
Inputs may be any that keep to these rules, and one draw needn't show every extreme that they name: `expert_ids`: within the 64 rows of one device no expert is named by more than 32 rows, and in every draw some expert is named by exactly 32 rows of some device.
All inputs are finite; a program needn't handle non-finite values.
Results may differ from the reference program's by a relative error of at most 0.0064.
Values may be sent and summed in bfloat16 or wider, within the bound.
No kernel may reach another device: no remote copies, remote signals or barrier semaphores. Data moves between devices by JAX's collectives and lax.ppermute only.
A program may use at most 128 MiB of HBM per device.

```python
import math
import jax
import jax.numpy as jnp
import numpy as np
from jax import lax

D = 1024
FF = 768
EXPERTS = 32
TOP = 8
TOK_DEV = 64
CAP = 32
TOKENS = 1024
N_EXPERT = 4
N_DP = 4


def levels(key, extent, shards, low, high):
    gain, own = 1.0, jax.random.fold_in(key, 6)
    for axis_at, blocks in shards:
        heights = jnp.exp(jax.random.uniform(jax.random.fold_in(own, axis_at), (blocks,), jnp.float32, low / len(shards), high / len(shards)))
        gain = gain * jnp.repeat(heights, extent[axis_at] // blocks).reshape([-1 if axis == axis_at else 1 for axis in range(len(extent))])
    return gain


def assign_block(rng, own, number, rows, count, top, most, lean):
    sequence = jax.random.permutation(rng, count)
    packed, ordinary = load_shares(count, rows * top, most, lean, True), load_shares(count, rows * top, most, lean, False)
    places = jnp.arange(count)

    def named(tallies, rotation):
        used = int((tallies > 0).sum())
        fixed = max(1, used // 4)
        passed = fixed + (places - fixed + rotation * (used - fixed)) % max(1, count - fixed)
        return jnp.zeros((count,), jnp.int32).at[sequence[jnp.where(places < fixed, places, passed)]].set(jnp.asarray(tallies, jnp.int32))

    tallies = jnp.where(number % 4 == 0, named(packed, number // 4), named(ordinary, number - number // 4 - 1))
    mixed = jax.random.permutation(jax.random.fold_in(own, 3), count)
    donor, taker = mixed[0:count // 2 * 2:2], mixed[1:count // 2 * 2:2]
    slack = jnp.minimum(tallies[donor] - 1, most - tallies[taker]) // 2
    slack = jnp.where((donor == sequence[0]) | (taker == sequence[0]) | (tallies[taker] == 0), 0, jnp.maximum(slack, 0))
    passed = jax.random.randint(jax.random.fold_in(own, 4), (count // 2,), 0, 1 << 20) % (slack + 1)
    tallies = tallies.at[donor].add(-passed).at[taker].add(passed)
    items = jnp.searchsorted(jnp.cumsum(tallies), jnp.arange(rows * top), side="right").astype(jnp.int32)
    table = items.reshape(top, rows).T
    table = table[jax.random.permutation(jax.random.fold_in(own, 1), rows)]
    rotation = jax.random.randint(jax.random.fold_in(own, 2), (rows, 1), 0, top)
    return jnp.take_along_axis(table, (jnp.arange(top)[None, :] + rotation) % top, axis=1)


def load_shares(amount, total, most, lean, full):
    loads = [(1 << 20) // math.isqrt(rank ** lean) + 1 for rank in range(1, amount + 1)]
    largest = most if full else min(most, max(-(-total // amount), total * loads[0] // sum(loads)))
    least = 1 if total - largest >= amount - 1 else 0
    holding, surplus = [largest] + [least] * (amount - 1), total - largest - least * (amount - 1)
    while surplus > 0:
        free = [i for i in range(1, amount) if holding[i] < largest] or [i for i in range(1, amount) if holding[i] < most]
        pool, remaining = sum([loads[i] for i in free]), surplus
        for i in free:
            addition = min(most - holding[i], max(1, remaining * loads[i] // pool), surplus)
            holding[i] = holding[i] + addition
            surplus = surplus - addition
    return np.array(holding)


def centred(own_key, dims, deviation, most, cuts=(), held_as=jnp.bfloat16):
    entries = deviation * jax.random.normal(own_key, dims, jnp.float32)
    if cuts:
        entries = entries * levels(own_key, dims, cuts, -0.22, 0.18)
    return jnp.clip(entries, -most, most).astype(held_as)


def setup_inputs(seed: int = 0, part: int = 0) -> dict:
    key_of = jax.random.split(jax.random.key(seed), 7)
    part_keys = jax.random.split(jax.random.fold_in(key_of[6], part), 7)
    tokens = centred(part_keys[0], (TOKENS, D), 1.0, 6.0, ((0, 16),))
    expert_ids_keys = jax.random.split(jax.random.fold_in(part_keys[1], 1), TOKENS // TOK_DEV)
    expert_ids_turns = jax.random.permutation(jax.random.fold_in(part_keys[1], 3), TOKENS // TOK_DEV)
    expert_ids = jax.vmap(lambda own, number: assign_block(jax.random.fold_in(part_keys[1], 2), own, number, TOK_DEV, EXPERTS, TOP, CAP, 2))(expert_ids_keys, expert_ids_turns).reshape((TOKENS, TOP))
    route_scores = jnp.clip(jnp.exp(math.log(1.0) - 2.9957323 * jax.random.uniform(part_keys[2], (TOKENS, TOP), jnp.float32) ** levels(part_keys[2], (TOKENS, TOP), ((0, 16),), -0.2, 0.2)), 0.05, 1.0)
    w_gate = centred(key_of[3], (EXPERTS, D, FF), D ** -0.5, 0.1875, ((0, 4),))
    w_up = centred(key_of[4], (EXPERTS, D, FF), D ** -0.5, 0.1875, ((0, 4),))
    w_down = centred(key_of[5], (EXPERTS, FF, D), FF ** -0.5, 0.21875, ((0, 4),))
    return dict(tokens=tokens, expert_ids=expert_ids, route_scores=route_scores, w_gate=w_gate, w_up=w_up, w_down=w_down)


def reference(tokens, expert_ids, route_scores, w_gate, w_up, w_down):
    token_total = tokens.shape[0]
    model_width = tokens.shape[1]
    slot_total = token_total * TOP
    most_rows = N_EXPERT * N_DP * CAP
    route_weights = (route_scores / jnp.sum(route_scores, axis=1, keepdims=True)).astype(jnp.bfloat16)
    flat_ids = expert_ids.reshape(slot_total).astype(jnp.int32)
    onehot = (flat_ids[:, None] == jnp.arange(EXPERTS, dtype=jnp.int32)[None, :]).astype(jnp.int32)
    slot_ranks = jnp.sum((jnp.cumsum(onehot, axis=0) - 1) * onehot, axis=1).astype(jnp.int32)
    slot_table = jnp.full((EXPERTS, most_rows), slot_total, jnp.int32)
    slot_table = slot_table.at[flat_ids, slot_ranks].set(jnp.arange(slot_total, dtype=jnp.int32))
    flat_weights = jnp.concatenate([route_weights.reshape(slot_total), jnp.zeros((1,), jnp.bfloat16)])
    padded_tokens = jnp.concatenate([tokens, jnp.zeros((1, model_width), jnp.bfloat16)], axis=0)
    highest = lax.Precision.HIGHEST

    def one_expert(totals, inputs):
        row_slots, gate_matrix, up_matrix, down_matrix = inputs
        token_rows = row_slots // TOP
        rows_in = padded_tokens[token_rows].astype(jnp.float32)
        gate_values = jnp.dot(rows_in, gate_matrix.astype(jnp.float32), precision=highest)
        up_values = jnp.dot(rows_in, up_matrix.astype(jnp.float32), precision=highest)
        hidden = (jax.nn.silu(gate_values) * up_values).astype(jnp.bfloat16)
        projected = jnp.dot(hidden.astype(jnp.float32), down_matrix.astype(jnp.float32), precision=highest)
        scaled = (flat_weights[row_slots].astype(jnp.float32)[:, None] * projected).astype(jnp.bfloat16)
        totals = totals.at[token_rows].add(scaled.astype(jnp.float32), mode="drop")
        return totals, None

    initial = jnp.zeros((token_total, model_width), jnp.float32)
    summed, unused = lax.scan(one_expert, initial, (slot_table, w_gate, w_up, w_down))
    return summed.astype(jnp.bfloat16)
```

```python
import functools

import jax
import jax.numpy as jnp
from jax import lax
from jax.experimental import pallas as pl
from jax.experimental.pallas import tpu as pltpu
from jax.sharding import PartitionSpec as P

GROUP = 4
DIRECT = 8


def expert_kernel(blocks, *refs):
    token_refs = refs[:blocks]
    meta_refs = refs[blocks : 2 * blocks]
    gate_ref, up_ref, down_ref = refs[2 * blocks : 2 * blocks + 3]
    out_refs = refs[2 * blocks + 3 : 3 * blocks + 3]
    rows_ref, meta_ref, total_ref = refs[3 * blocks + 3 :]
    count = token_refs[0].shape[0]
    local_experts = gate_ref.shape[0]
    top = meta_ref.shape[1] // 2
    for index in range(blocks):
        span = pl.ds(index * count, count)
        rows_ref[span, :] = token_refs[index][...]
        meta_ref[span, :] = meta_refs[index][...]
    first = lax.axis_index("expert") * local_experts

    def one_expert(member, carry):
        rows = rows_ref[...]
        gate = jnp.dot(rows, gate_ref[member], preferred_element_type=jnp.float32)
        up = jnp.dot(rows, up_ref[member], preferred_element_type=jnp.float32)
        hidden = (gate / (1.0 + jnp.exp(-gate)) * up).astype(jnp.bfloat16)
        projected = jnp.dot(hidden, down_ref[member], preferred_element_type=jnp.float32)
        named = meta_ref[:, :top] == (first + member).astype(jnp.float32)
        weight = jnp.sum(jnp.where(named, meta_ref[:, top:], 0.0), axis=1, keepdims=True)
        scaled = weight * projected

        @pl.when(member == 0)
        def _():
            total_ref[...] = scaled

        @pl.when(member > 0)
        def _():
            total_ref[...] += scaled

        return carry

    lax.fori_loop(0, local_experts, one_expert, 0)
    for index in range(blocks):
        span = pl.ds(index * count, count)
        out_refs[index][...] = total_ref[span, :].astype(out_refs[index].dtype)


def run_experts(tokens, metas, weights, own_first):
    blocks = len(tokens)
    count, width = tokens[0].shape
    whole = pl.BlockSpec(memory_space=pltpu.VMEM)
    kinds = [jnp.float32 if own_first and index == 0 else jnp.bfloat16 for index in range(blocks)]
    rows = blocks * count
    flops = 6 * rows * weights[0].size
    moved = sum(2 * w.size for w in weights)
    return pl.pallas_call(
        functools.partial(expert_kernel, blocks),
        out_shape=[jax.ShapeDtypeStruct((count, width), kind) for kind in kinds],
        in_specs=[whole] * (2 * blocks + 3),
        out_specs=[whole] * blocks,
        scratch_shapes=[
            pltpu.VMEM((rows, width), jnp.bfloat16),
            pltpu.VMEM((rows, metas[0].shape[1]), jnp.float32),
            pltpu.VMEM((rows, width), jnp.float32),
        ],
        compiler_params=pltpu.CompilerParams(vmem_limit_bytes=20 << 20),
        cost_estimate=pl.CostEstimate(flops=flops, bytes_accessed=moved, transcendentals=0),
    )(*tokens, *metas, *weights)


def per_device(tokens, expert_ids, route_scores, w_gate, w_up, w_down):
    peers = lax.axis_size("expert")
    weights = (w_gate, w_up, w_down)
    route_weights = (route_scores / jnp.sum(route_scores, axis=1, keepdims=True)).astype(
        jnp.bfloat16
    )
    meta = jnp.concatenate(
        [expert_ids.astype(jnp.float32), route_weights.astype(jnp.float32)], axis=1
    )
    if peers <= DIRECT and peers & (peers - 1) == 0:
        order = sorted(range(1, peers), key=lambda shift: (-(shift & -shift), shift))
        pairs = {shift: [(i, i ^ shift) for i in range(peers)] for shift in order}
        got = [lax.ppermute(tokens, "expert", pairs[shift]) for shift in order]
        got_meta = [lax.ppermute(meta, "expert", pairs[shift]) for shift in order]
        parts = run_experts([tokens, *got], [meta, *got_meta], weights, True)
        back = [lax.ppermute(p, "expert", pairs[s]) for p, s in zip(parts[1:], order)]
        total = parts[0]
        for part in back:
            total = total + part.astype(jnp.float32)
        return total.astype(jnp.bfloat16)
    got = lax.all_gather(tokens, "expert")
    got_meta = lax.all_gather(meta, "expert")
    parts = []
    for start in range(0, peers, GROUP):
        here = range(start, min(start + GROUP, peers))
        parts += run_experts([got[i] for i in here], [got_meta[i] for i in here], weights, False)
    back = lax.all_to_all(jnp.stack(parts), "expert", 0, 0, tiled=True)
    return jnp.sum(back.astype(jnp.float32), axis=0).astype(jnp.bfloat16)


def solution(mesh):
    split = P(("groups", "expert", "dp"), None)
    held = P("expert", None, None)
    return jax.shard_map(
        per_device,
        mesh=mesh,
        in_specs=(split, split, split, held, held, held),
        out_specs=split,
        check_vma=False,
    )
```

```python
import functools

import jax
import jax.numpy as jnp
from jax import lax
from jax.experimental import pallas as pl
from jax.experimental.pallas import tpu as pltpu
from jax.sharding import PartitionSpec as P

LANES = 128
GROUP = 4
DIRECT = 8
MIB = 1 << 20
VMEM = pl.BlockSpec(memory_space=pltpu.VMEM)
ANY = pl.BlockSpec(memory_space=pl.ANY)


def in_hbm(array):
    return pltpu.with_memory_space_constraint(array, pltpu.HBM)


def hidden_of(rows, gate_matrix, up_matrix):
    gate = jnp.dot(rows, gate_matrix, preferred_element_type=jnp.float32)
    up = jnp.dot(rows, up_matrix, preferred_element_type=jnp.float32)
    return (gate / (1.0 + jnp.exp(-gate)) * up).astype(jnp.bfloat16)


def weight_of(spread, expert):
    lane = lax.broadcasted_iota(jnp.int32, spread.shape, 1)
    return jnp.sum(jnp.where(lane == expert, spread, 0.0), axis=1, keepdims=True)


def pack_kernel(token_ref, id_ref, score_ref, out_ref):
    width = token_ref.shape[1]
    out_ref[:, :width] = token_ref[...]
    scores = score_ref[...]
    shares = (scores / jnp.sum(scores, axis=0, keepdims=True)).astype(jnp.bfloat16)
    shares = shares.astype(jnp.float32)
    ids = id_ref[...]
    expert = lax.broadcasted_iota(jnp.int32, (out_ref.shape[1] - width, ids.shape[1]), 0)
    spread = jnp.zeros(expert.shape, jnp.float32)
    for slot in range(ids.shape[0]):
        spread += jnp.where(expert == ids[slot : slot + 1], shares[slot : slot + 1], 0.0)
    out_ref[:, width:] = spread.T.astype(jnp.bfloat16)


def pack(tokens, expert_ids, route_scores, experts):
    count, width = tokens.shape
    wide = width + -(-experts // LANES) * LANES
    return pl.pallas_call(
        pack_kernel,
        out_shape=jax.ShapeDtypeStruct((count, wide), jnp.bfloat16),
        in_specs=[VMEM] * 3,
        out_specs=VMEM,
        compiler_params=pltpu.CompilerParams(vmem_limit_bytes=4 * MIB),
    )(tokens, expert_ids.T, route_scores.T)


def own_kernel(packed_ref, gate_hbm, up_hbm, gate_ref, up_ref, hidden_ref, sems):
    local_experts, width, _ = gate_ref.shape

    def load(member, which):
        source, target = ((gate_hbm, gate_ref), (up_hbm, up_ref))[which]
        return pltpu.make_async_copy(
            source.at[member], target.at[member], sems.at[which, member]
        )

    for member in range(local_experts):
        load(member, 0).start()
        load(member, 1).start()

    def one_expert(member, carry):
        load(member, 0).wait()
        load(member, 1).wait()
        rows = packed_ref[:, :width]
        hidden_ref[member] = hidden_of(rows, gate_ref[member], up_ref[member])
        return carry

    lax.fori_loop(0, local_experts, one_expert, 0)


def own_hidden(packed, w_gate, w_up):
    local_experts, width, units = w_gate.shape
    count = packed.shape[0]
    return pl.pallas_call(
        own_kernel,
        out_shape=[
            pltpu.VMEM(w_gate.shape, w_gate.dtype),
            pltpu.VMEM(w_up.shape, w_up.dtype),
            pltpu.VMEM((local_experts, count, units), jnp.bfloat16),
        ],
        in_specs=[VMEM, ANY, ANY],
        out_specs=[VMEM] * 3,
        scratch_shapes=[pltpu.SemaphoreType.DMA((2, local_experts))],
        compiler_params=pltpu.CompilerParams(vmem_limit_bytes=8 * MIB),
        cost_estimate=pl.CostEstimate(
            flops=4 * count * w_gate.size, bytes_accessed=4 * w_gate.size, transcendentals=0
        ),
    )(packed, in_hbm(w_gate), in_hbm(w_up))


def rest_kernel(blocks, *refs):
    packed_refs = refs[:blocks]
    gate_ref, up_ref, own_ref, down_hbm = refs[blocks : blocks + 4]
    out_refs = refs[blocks + 4 : 2 * blocks + 4]
    rows_ref, spread_ref, down_ref, total_ref, sems = refs[2 * blocks + 4 :]
    local_experts, width, _ = gate_ref.shape
    count = packed_refs[0].shape[0]

    def load(member):
        return pltpu.make_async_copy(down_hbm.at[member], down_ref.at[member], sems.at[member])

    for member in range(local_experts):
        load(member).start()
    for index in range(blocks):
        span = pl.ds(index * count, count)
        if index:
            rows_ref[pl.ds((index - 1) * count, count), :] = packed_refs[index][:, :width]
        spread_ref[span, :] = packed_refs[index][:, width:].astype(jnp.float32)
    first = lax.axis_index("expert") * local_experts

    def one_expert(member, carry):
        hidden = hidden_of(rows_ref[...], gate_ref[member], up_ref[member])
        hidden = jnp.concatenate([own_ref[member], hidden], axis=0)
        load(member).wait()
        projected = jnp.dot(hidden, down_ref[member], preferred_element_type=jnp.float32)
        scaled = weight_of(spread_ref[...], first + member) * projected

        @pl.when(member == 0)
        def _():
            total_ref[...] = scaled

        @pl.when(member > 0)
        def _():
            total_ref[...] += scaled

        return carry

    lax.fori_loop(0, local_experts, one_expert, 0)
    for index in range(blocks):
        span = pl.ds(index * count, count)
        out_refs[index][...] = total_ref[span, :].astype(out_refs[index].dtype)


def rest(packed, gate, up, own, w_down):
    blocks = len(packed)
    count = packed[0].shape[0]
    local_experts, units, width = w_down.shape
    rows = blocks * count
    return pl.pallas_call(
        functools.partial(rest_kernel, blocks),
        out_shape=[
            jax.ShapeDtypeStruct((count, width), jnp.bfloat16 if index else jnp.float32)
            for index in range(blocks)
        ],
        in_specs=[VMEM] * (blocks + 3) + [ANY],
        out_specs=[VMEM] * blocks,
        scratch_shapes=[
            pltpu.VMEM((rows - count, width), jnp.bfloat16),
            pltpu.VMEM((rows, packed[0].shape[1] - width), jnp.float32),
            pltpu.VMEM(w_down.shape, w_down.dtype),
            pltpu.VMEM((rows, width), jnp.float32),
            pltpu.SemaphoreType.DMA((local_experts,)),
        ],
        compiler_params=pltpu.CompilerParams(vmem_limit_bytes=26 * MIB),
        cost_estimate=pl.CostEstimate(
            flops=6 * rows * w_down.size, bytes_accessed=2 * w_down.size, transcendentals=0
        ),
    )(*packed, gate, up, own, in_hbm(w_down))


def per_device(tokens, expert_ids, route_scores, w_gate, w_up, w_down):
    peers = lax.axis_size("expert")
    packed = pack(tokens, expert_ids, route_scores, peers * w_gate.shape[0])
    if peers <= DIRECT and peers & (peers - 1) == 0:
        order = sorted(range(1, peers), key=lambda shift: (-(shift & -shift), shift))
        pairs = {shift: [(i, i ^ shift) for i in range(peers)] for shift in order}
        got = [lax.ppermute(packed, "expert", pairs[shift]) for shift in order]
        gate, up, own = own_hidden(packed, w_gate, w_up)
        parts = rest([packed, *got], gate, up, own, w_down)
        back = [lax.ppermute(p, "expert", pairs[s]) for p, s in zip(parts[1:], order)]
        total = parts[0]
        for part in back:
            total = total + part.astype(jnp.float32)
        return total.astype(jnp.bfloat16)
    got = lax.all_gather(packed, "expert")
    parts = []
    for start in range(0, peers, GROUP):
        here = [got[i] for i in range(start, min(start + GROUP, peers))]
        gate, up, own = own_hidden(here[0], w_gate, w_up)
        parts += rest(here, gate, up, own, w_down)
    parts = [part.astype(jnp.bfloat16) for part in parts]
    back = lax.all_to_all(jnp.stack(parts), "expert", 0, 0, tiled=True)
    return jnp.sum(back.astype(jnp.float32), axis=0).astype(jnp.bfloat16)


def solution(mesh):
    split = P(("groups", "expert", "dp"), None)
    held = P("expert", None, None)
    return jax.shard_map(
        per_device,
        mesh=mesh,
        in_specs=(split, split, split, held, held, held),
        out_specs=split,
        check_vma=False,
    )
```

```python
import functools

import jax
import jax.numpy as jnp
from jax import lax
from jax.experimental import pallas as pl
from jax.experimental.pallas import tpu as pltpu
from jax.sharding import PartitionSpec as P

SUBLANES, LANES = 8, 128
CHUNK = 256
GROUP = 4
DIRECT = 8
MIB = 1 << 20
VMEM = pl.BlockSpec(memory_space=pltpu.VMEM)
ANY = pl.BlockSpec(memory_space=pl.ANY)


def in_hbm(array):
    return pltpu.with_memory_space_constraint(array, pltpu.HBM)


def hidden_of(rows, gate_matrix, up_matrix):
    gate = jnp.dot(rows, gate_matrix, preferred_element_type=jnp.float32)
    up = jnp.dot(rows, up_matrix, preferred_element_type=jnp.float32)
    return (gate / (1.0 + jnp.exp(-gate)) * up).astype(jnp.bfloat16)


def tiles_of(array):
    rows, width = array.shape
    split = array.reshape(rows // SUBLANES, SUBLANES, width // LANES, LANES)
    return split.transpose(0, 2, 1, 3).reshape(-1, SUBLANES, LANES)


def pack_kernel(tile_hbm, id_hbm, score_hbm, out_ref, id_ref, score_ref, sems):
    tiles = tile_hbm.shape[0]
    copies = [
        pltpu.make_async_copy(id_hbm, id_ref, sems.at[0]),
        pltpu.make_async_copy(score_hbm, score_ref, sems.at[1]),
        pltpu.make_async_copy(tile_hbm, out_ref.at[pl.ds(0, tiles)], sems.at[2]),
    ]
    for copy in copies:
        copy.start()
    out_ref[tiles] = jnp.zeros((SUBLANES, LANES), jnp.bfloat16)
    out_ref[tiles + 1] = jnp.zeros((SUBLANES, LANES), jnp.bfloat16)
    top, count = id_ref.shape
    copies[0].wait()
    copies[1].wait()
    scores = score_ref[...]
    shares = scores / jnp.sum(scores, axis=0, keepdims=True)
    out_ref[tiles, :top, :count] = id_ref[...].astype(jnp.float32).astype(jnp.bfloat16)
    out_ref[tiles + 1, :top, :count] = shares.astype(jnp.bfloat16)
    copies[2].wait()


def pack(tokens, expert_ids, route_scores):
    tiles = tiles_of(tokens)
    count, top = expert_ids.shape
    return pl.pallas_call(
        pack_kernel,
        out_shape=pltpu.VMEM((tiles.shape[0] + 2, SUBLANES, LANES), jnp.bfloat16),
        in_specs=[ANY] * 3,
        out_specs=VMEM,
        scratch_shapes=[
            pltpu.VMEM((top, count), jnp.int32),
            pltpu.VMEM((top, count), jnp.float32),
            pltpu.SemaphoreType.DMA((3,)),
        ],
        compiler_params=pltpu.CompilerParams(vmem_limit_bytes=4 * MIB),
    )(in_hbm(tiles), in_hbm(expert_ids.T), in_hbm(route_scores.T))


def own_kernel(token_hbm, gate_hbm, up_hbm, gate_ref, up_ref, hidden_ref, rows_ref, sems):
    local_experts = gate_ref.shape[0]
    tokens = pltpu.make_async_copy(token_hbm, rows_ref, sems.at[2, 0])
    tokens.start()

    def load(member, which):
        source, target = ((gate_hbm, gate_ref), (up_hbm, up_ref))[which]
        return pltpu.make_async_copy(
            source.at[member], target.at[member], sems.at[which, member]
        )

    for member in range(local_experts):
        load(member, 0).start()
        load(member, 1).start()
    tokens.wait()

    def one_expert(member, carry):
        load(member, 0).wait()
        load(member, 1).wait()
        hidden_ref[member] = hidden_of(rows_ref[...], gate_ref[member], up_ref[member])
        return carry

    lax.fori_loop(0, local_experts, one_expert, 0)


def own_hidden(tokens, w_gate, w_up):
    local_experts, width, units = w_gate.shape
    count = tokens.shape[0]
    return pl.pallas_call(
        own_kernel,
        out_shape=[
            pltpu.VMEM(w_gate.shape, w_gate.dtype),
            pltpu.VMEM(w_up.shape, w_up.dtype),
            pltpu.VMEM((local_experts, count, units), jnp.bfloat16),
        ],
        in_specs=[ANY] * 3,
        out_specs=[VMEM] * 3,
        scratch_shapes=[
            pltpu.VMEM(tokens.shape, tokens.dtype),
            pltpu.SemaphoreType.DMA((3, local_experts)),
        ],
        compiler_params=pltpu.CompilerParams(vmem_limit_bytes=8 * MIB),
        cost_estimate=pl.CostEstimate(
            flops=4 * count * w_gate.size, bytes_accessed=4 * w_gate.size, transcendentals=0
        ),
    )(in_hbm(tokens), in_hbm(w_gate), in_hbm(w_up))


def rest_kernel(blocks, top, *refs):
    packed_refs = refs[:blocks]
    gate_ref, up_ref, own_ref, down_hbm = refs[blocks : blocks + 4]
    out_refs = refs[blocks + 4 : 2 * blocks + 4]
    rows_ref, spread_ref, hidden_ref, down_ref, total_ref, sems = refs[2 * blocks + 4 :]
    local_experts, width, units = gate_ref.shape
    count = own_ref.shape[1]
    across = width // LANES
    tiles = packed_refs[0].shape[0] - 2

    def load(member):
        return pltpu.make_async_copy(down_hbm.at[member], down_ref.at[member], sems.at[member])

    for member in range(local_experts):
        load(member).start()
    for index in range(1, blocks):
        for tile in range(tiles):
            row = (index - 1) * count + tile // across * SUBLANES
            column = tile % across * LANES
            rows_ref[row : row + SUBLANES, column : column + LANES] = packed_refs[index][tile]
    held = spread_ref.shape[1]
    first = lax.axis_index("expert") * local_experts
    expert = lax.broadcasted_iota(jnp.int32, (held, count), 0) + first
    for index in range(blocks):
        ids = packed_refs[index][tiles].astype(jnp.float32).astype(jnp.int32)
        shares = packed_refs[index][tiles + 1].astype(jnp.float32)
        spread = jnp.zeros((held, count), jnp.float32)
        for slot in range(top):
            named = expert == ids[slot : slot + 1, :count]
            spread += jnp.where(named, shares[slot : slot + 1, :count], 0.0)
        spread_ref[index * count : (index + 1) * count, :] = spread.T

    def fill(member):
        hidden_ref[member % 2, :count, :] = own_ref[member]
        for start in range(0, units, CHUNK):
            span = slice(start, min(start + CHUNK, units))
            hidden_ref[member % 2, count:, span] = hidden_of(
                rows_ref[...], gate_ref[member, :, span], up_ref[member, :, span]
            )

    def project(member):
        load(member).wait()
        weight = spread_ref[:, member : member + 1]
        for start in range(0, width, CHUNK):
            span = slice(start, min(start + CHUNK, width))
            scaled = weight * jnp.dot(
                hidden_ref[member % 2],
                down_ref[member, :, span],
                preferred_element_type=jnp.float32,
            )
            if member:
                scaled = total_ref[:, span] + scaled
            if member < local_experts - 1:
                total_ref[:, span] = scaled
                continue
            for index in range(blocks):
                part = scaled[index * count : (index + 1) * count]
                out_refs[index][:, span] = part.astype(out_refs[index].dtype)

    fill(0)
    for member in range(local_experts):
        if member + 1 < local_experts:
            fill(member + 1)
        project(member)


def rest(packed, gate, up, own, w_down, top):
    blocks = len(packed)
    local_experts, units, width = w_down.shape
    count = own.shape[1]
    rows = blocks * count
    return pl.pallas_call(
        functools.partial(rest_kernel, blocks, top),
        out_shape=[
            jax.ShapeDtypeStruct((count, width), jnp.bfloat16 if index else jnp.float32)
            for index in range(blocks)
        ],
        in_specs=[VMEM] * (blocks + 3) + [ANY],
        out_specs=[VMEM] * blocks,
        scratch_shapes=[
            pltpu.VMEM((rows - count, width), jnp.bfloat16),
            pltpu.VMEM((rows, -(-local_experts // SUBLANES) * SUBLANES), jnp.float32),
            pltpu.VMEM((2, rows, units), jnp.bfloat16),
            pltpu.VMEM(w_down.shape, w_down.dtype),
            pltpu.VMEM((rows, width), jnp.float32),
            pltpu.SemaphoreType.DMA((local_experts,)),
        ],
        compiler_params=pltpu.CompilerParams(vmem_limit_bytes=26 * MIB),
        cost_estimate=pl.CostEstimate(
            flops=6 * rows * w_down.size, bytes_accessed=2 * w_down.size, transcendentals=0
        ),
    )(*packed, gate, up, own, in_hbm(w_down))


def per_device(tokens, expert_ids, route_scores, w_gate, w_up, w_down):
    peers = lax.axis_size("expert")
    top = expert_ids.shape[1]
    packed = pack(tokens, expert_ids, route_scores)
    if peers <= DIRECT and peers & (peers - 1) == 0:
        order = sorted(range(1, peers), key=lambda shift: (-(shift & -shift), shift))
        pairs = {shift: [(i, i ^ shift) for i in range(peers)] for shift in order}
        got = [lax.ppermute(packed, "expert", pairs[shift]) for shift in order]
        gate, up, own = own_hidden(tokens, w_gate, w_up)
        parts = rest([packed, *got], gate, up, own, w_down, top)
        back = [lax.ppermute(p, "expert", pairs[s]) for p, s in zip(parts[1:], order)]
        total = parts[0]
        for part in back:
            total = total + part.astype(jnp.float32)
        return total.astype(jnp.bfloat16)
    got = lax.all_gather(packed, "expert")
    every = lax.all_gather(tokens, "expert")
    parts = []
    for start in range(0, peers, GROUP):
        here = [got[i] for i in range(start, min(start + GROUP, peers))]
        gate, up, own = own_hidden(every[start], w_gate, w_up)
        parts += rest(here, gate, up, own, w_down, top)
    parts = [part.astype(jnp.bfloat16) for part in parts]
    back = lax.all_to_all(jnp.stack(parts), "expert", 0, 0, tiled=True)
    return jnp.sum(back.astype(jnp.float32), axis=0).astype(jnp.bfloat16)


def solution(mesh):
    split = P(("groups", "expert", "dp"), None)
    held = P("expert", None, None)
    return jax.shard_map(
        per_device,
        mesh=mesh,
        in_specs=(split, split, split, held, held, held),
        out_specs=split,
        check_vma=False,
    )
```

```python
import functools

import jax
import jax.numpy as jnp
from jax import lax
from jax.experimental import pallas as pl
from jax.experimental.pallas import tpu as pltpu
from jax.sharding import PartitionSpec as P


SUBLANES, LANES = 8, 128
CHUNK = 256
GROUP = 4
MIB = 1 << 20
VMEM = pl.BlockSpec(memory_space=pltpu.VMEM)
ANY = pl.BlockSpec(memory_space=pl.ANY)


def slots_of(experts):
    return -(-experts // SUBLANES) * SUBLANES


def in_hbm(array):
    return pltpu.with_memory_space_constraint(array, pltpu.HBM)


def hidden_of(rows, gate_matrix, up_matrix):
    gate = jnp.dot(rows, gate_matrix, preferred_element_type=jnp.float32)
    up = jnp.dot(rows, up_matrix, preferred_element_type=jnp.float32)
    return (gate / (1.0 + jnp.exp(-gate)) * up).astype(jnp.bfloat16)


def tiles_of(array):
    rows, width = array.shape
    split = array.reshape(rows // SUBLANES, SUBLANES, width // LANES, LANES)
    return split.transpose(0, 2, 1, 3).reshape(-1, SUBLANES, LANES)


def pack_kernel(tile_hbm, id_hbm, score_hbm, out_ref, id_ref, score_ref, sems):
    tiles = tile_hbm.shape[0]
    copies = [
        pltpu.make_async_copy(id_hbm, id_ref, sems.at[0]),
        pltpu.make_async_copy(score_hbm, score_ref, sems.at[1]),
        pltpu.make_async_copy(tile_hbm, out_ref.at[pl.ds(0, tiles)], sems.at[2]),
    ]
    for copy in copies:
        copy.start()
    out_ref[tiles] = jnp.zeros((SUBLANES, LANES), jnp.bfloat16)
    out_ref[tiles + 1] = jnp.zeros((SUBLANES, LANES), jnp.bfloat16)
    top, count = id_ref.shape
    copies[0].wait()
    copies[1].wait()
    scores = score_ref[...]
    shares = scores / jnp.sum(scores, axis=0, keepdims=True)
    out_ref[tiles, :top, :count] = id_ref[...].astype(jnp.float32).astype(jnp.bfloat16)
    out_ref[tiles + 1, :top, :count] = shares.astype(jnp.bfloat16)
    copies[2].wait()


def pack(tokens, expert_ids, route_scores):
    tiles = tiles_of(tokens)
    count, top = expert_ids.shape
    return pl.pallas_call(
        pack_kernel,
        out_shape=pltpu.VMEM((tiles.shape[0] + 2, SUBLANES, LANES), jnp.bfloat16),
        in_specs=[ANY] * 3,
        out_specs=VMEM,
        scratch_shapes=[
            pltpu.VMEM((top, count), jnp.int32),
            pltpu.VMEM((top, count), jnp.float32),
            pltpu.SemaphoreType.DMA((3,)),
        ],
        compiler_params=pltpu.CompilerParams(vmem_limit_bytes=4 * MIB),
    )(in_hbm(tiles), in_hbm(expert_ids.T), in_hbm(route_scores.T))


def own_kernel(token_hbm, gate_hbm, up_hbm, gate_ref, up_ref, hidden_ref, rows_ref, sems):
    local_experts = gate_ref.shape[0]
    tokens = pltpu.make_async_copy(token_hbm, rows_ref, sems.at[2, 0])
    tokens.start()

    def load(member, which):
        source, target = ((gate_hbm, gate_ref), (up_hbm, up_ref))[which]
        return pltpu.make_async_copy(
            source.at[member], target.at[member], sems.at[which, member]
        )

    for member in range(local_experts):
        load(member, 0).start()
        load(member, 1).start()
    tokens.wait()

    def one_expert(member, carry):
        load(member, 0).wait()
        load(member, 1).wait()
        hidden_ref[member] = hidden_of(rows_ref[...], gate_ref[member], up_ref[member])
        return carry

    lax.fori_loop(0, local_experts, one_expert, 0)


def own_hidden(tokens, w_gate, w_up):
    local_experts, _, units = w_gate.shape
    count = tokens.shape[0]
    return pl.pallas_call(
        own_kernel,
        out_shape=[
            pltpu.VMEM(w_gate.shape, w_gate.dtype),
            pltpu.VMEM(w_up.shape, w_up.dtype),
            pltpu.VMEM((local_experts, count, units), jnp.bfloat16),
        ],
        in_specs=[ANY] * 3,
        out_specs=[VMEM] * 3,
        scratch_shapes=[
            pltpu.VMEM(tokens.shape, tokens.dtype),
            pltpu.SemaphoreType.DMA((3, local_experts)),
        ],
        compiler_params=pltpu.CompilerParams(vmem_limit_bytes=8 * MIB),
        cost_estimate=pl.CostEstimate(
            flops=4 * count * w_gate.size, bytes_accessed=4 * w_gate.size, transcendentals=0
        ),
    )(in_hbm(tokens), in_hbm(w_gate), in_hbm(w_up))


def spread_shares(packed_refs, spread_ref, count, top, held):
    first = lax.axis_index("expert") * held
    slots = spread_ref.shape[1]
    expert = lax.broadcasted_iota(jnp.int32, (slots, count), 0) + first
    for index, packed_ref in enumerate(packed_refs):
        tiles = packed_ref.shape[0] - 2
        ids = packed_ref[tiles].astype(jnp.float32).astype(jnp.int32)
        shares = packed_ref[tiles + 1].astype(jnp.float32)
        spread = jnp.zeros((slots, count), jnp.float32)
        for slot in range(top):
            named = expert == ids[slot : slot + 1, :count]
            spread += jnp.where(named, shares[slot : slot + 1, :count], 0.0)
        spread_ref[index * count : (index + 1) * count, :] = spread.T


def project_into(out_refs, total_ref, spread_ref, down_ref, hidden_at, count):
    local_experts, _, width = down_ref.shape
    for member in range(local_experts):
        weight = spread_ref[:, member : member + 1]
        for start in range(0, width, CHUNK):
            span = slice(start, min(start + CHUNK, width))
            scaled = weight * jnp.dot(
                hidden_at(member), down_ref[member, :, span], preferred_element_type=jnp.float32
            )
            if member:
                scaled = total_ref[:, span] + scaled
            if member < local_experts - 1:
                total_ref[:, span] = scaled
                continue
            for index, out_ref in enumerate(out_refs):
                part = scaled[index * count : (index + 1) * count]
                out_ref[:, span] = part.astype(out_ref.dtype)


def far_kernel(blocks, sent, top, *refs):
    packed_refs = refs[:blocks]
    gate_ref, up_ref, down_hbm = refs[blocks : blocks + 3]
    outs = refs[blocks + 3 :]
    out_refs, down_ref, near_ref = outs[:sent], outs[sent], outs[sent + 1]
    rows_ref, spread_ref, hidden_ref, total_ref, sems = outs[sent + 2 :]
    local_experts, width, units = gate_ref.shape
    count = rows_ref.shape[0] // blocks
    across = width // LANES
    tiles = packed_refs[0].shape[0] - 2
    loads = [
        pltpu.make_async_copy(down_hbm.at[member], down_ref.at[member], sems.at[member])
        for member in range(local_experts)
    ]
    for load in loads:
        load.start()
    for index in range(blocks):
        for tile in range(tiles):
            row = index * count + tile // across * SUBLANES
            column = tile % across * LANES
            rows_ref[row : row + SUBLANES, column : column + LANES] = packed_refs[index][tile]
    spread_shares(packed_refs[:sent], spread_ref, count, top, local_experts)
    for member in range(local_experts):
        for start in range(0, units, CHUNK):
            span = slice(start, min(start + CHUNK, units))
            hidden = hidden_of(rows_ref[...], gate_ref[member, :, span], up_ref[member, :, span])
            hidden_ref[member, :, span] = hidden[: sent * count]
            if sent < blocks:
                near_ref[member, :, span] = hidden[sent * count :]
    for load in loads:
        load.wait()
    project_into(
        out_refs, total_ref, spread_ref, down_ref, lambda member: hidden_ref[member], count
    )


def far(packed, sent, gate, up, w_down, count, top):
    blocks = len(packed)
    local_experts, units, width = w_down.shape
    rows = blocks * count
    near_rows = max(rows - sent * count, SUBLANES)
    *parts, down, near_hidden = pl.pallas_call(
        functools.partial(far_kernel, blocks, sent, top),
        out_shape=[jax.ShapeDtypeStruct((count, width), jnp.bfloat16)] * sent
        + [
            pltpu.VMEM(w_down.shape, w_down.dtype),
            pltpu.VMEM((local_experts, near_rows, units), jnp.bfloat16),
        ],
        in_specs=[VMEM] * (blocks + 2) + [ANY],
        out_specs=[VMEM] * (sent + 2),
        scratch_shapes=[
            pltpu.VMEM((rows, width), jnp.bfloat16),
            pltpu.VMEM((sent * count, slots_of(local_experts)), jnp.float32),
            pltpu.VMEM((local_experts, sent * count, units), jnp.bfloat16),
            pltpu.VMEM((sent * count, width), jnp.float32),
            pltpu.SemaphoreType.DMA((local_experts,)),
        ],
        compiler_params=pltpu.CompilerParams(vmem_limit_bytes=12 * MIB),
        cost_estimate=pl.CostEstimate(
            flops=6 * rows * w_down.size, bytes_accessed=2 * w_down.size, transcendentals=0
        ),
    )(*packed, gate, up, in_hbm(w_down))
    return parts, down, near_hidden


def near_kernel(top, *refs):
    packed_refs, hidden_refs, down_ref = refs[:2], refs[2:4], refs[4]
    out_refs = refs[5:7]
    spread_ref, hidden_ref, total_ref = refs[7:]
    count = hidden_refs[0].shape[1]
    spread_shares(packed_refs, spread_ref, count, top, down_ref.shape[0])
    hidden_ref[:, :count, :] = hidden_refs[0][...]
    hidden_ref[:, count:, :] = hidden_refs[1][...]
    project_into(
        out_refs, total_ref, spread_ref, down_ref, lambda member: hidden_ref[member], count
    )


def near(packed, hiddens, down, top):
    local_experts, count, units = hiddens[0].shape
    width = down.shape[2]
    return pl.pallas_call(
        functools.partial(near_kernel, top),
        out_shape=[
            jax.ShapeDtypeStruct((count, width), jnp.float32),
            jax.ShapeDtypeStruct((count, width), jnp.bfloat16),
        ],
        in_specs=[VMEM] * 5,
        out_specs=[VMEM] * 2,
        scratch_shapes=[
            pltpu.VMEM((2 * count, slots_of(local_experts)), jnp.float32),
            pltpu.VMEM((local_experts, 2 * count, units), jnp.bfloat16),
            pltpu.VMEM((2 * count, width), jnp.float32),
        ],
        compiler_params=pltpu.CompilerParams(vmem_limit_bytes=8 * MIB),
        cost_estimate=pl.CostEstimate(
            flops=4 * count * down.size, bytes_accessed=2 * down.size, transcendentals=0
        ),
    )(*packed, *hiddens, down)


def exchange(array, pairs):
    return lax.ppermute(array, "expert", pairs)


def per_device(tokens, expert_ids, route_scores, w_gate, w_up, w_down):
    peers = lax.axis_size("expert")
    count, top = expert_ids.shape
    packed = pack(tokens, expert_ids, route_scores)
    if peers == 4:
        pairs = {shift: [(i, i ^ shift) for i in range(peers)] for shift in (2, 3, 1)}
        got = {s: exchange(packed, pairs[s]) for s in pairs}
        gate, up, own = own_hidden(tokens, w_gate, w_up)
        parts, down, beside = far([got[2], got[3], got[1]], 2, gate, up, w_down, count, top)
        back = [exchange(part, pairs[s]) for part, s in zip(parts, (2, 3))]
        total, part = near([packed, got[1]], [own, beside], down, top)
        back.append(exchange(part, pairs[1]))
        for part in back:
            total = total + part.astype(jnp.float32)
        return total.astype(jnp.bfloat16)
    got = lax.all_gather(packed, "expert")
    gate, up, _ = own_hidden(tokens, w_gate, w_up)
    parts = []
    for start in range(0, peers, GROUP):
        here = [got[i] for i in range(start, min(start + GROUP, peers))]
        parts += far(here, len(here), gate, up, w_down, count, top)[0]
    back = lax.all_to_all(jnp.stack(parts), "expert", 0, 0, tiled=True)
    return jnp.sum(back.astype(jnp.float32), axis=0).astype(jnp.bfloat16)


def solution(mesh):
    split = P(("groups", "expert", "dp"), None)
    held = P("expert", None, None)
    return jax.shard_map(
        per_device,
        mesh=mesh,
        in_specs=(split, split, split, held, held, held),
        out_specs=split,
        check_vma=False,
    )
```

```python
import functools

import jax
import jax.numpy as jnp
from jax import lax
from jax.experimental import pallas as pl
from jax.experimental.pallas import tpu as pltpu
from jax.sharding import PartitionSpec as P


SUBLANES, LANES = 8, 128
CHUNK = 256
GROUP = 4
MIB = 1 << 20
VMEM = pl.BlockSpec(memory_space=pltpu.VMEM)
ANY = pl.BlockSpec(memory_space=pl.ANY)


def slots_of(experts):
    return -(-experts // SUBLANES) * SUBLANES


def in_hbm(array):
    return pltpu.with_memory_space_constraint(array, pltpu.HBM)


def hidden_of(rows, gate_matrix, up_matrix):
    gate = jnp.dot(rows, gate_matrix, preferred_element_type=jnp.float32)
    up = jnp.dot(rows, up_matrix, preferred_element_type=jnp.float32)
    return (gate / (1.0 + jnp.exp(-gate)) * up).astype(jnp.bfloat16)


def tiles_of(array):
    rows, width = array.shape
    split = array.reshape(rows // SUBLANES, SUBLANES, width // LANES, LANES)
    return split.transpose(0, 2, 1, 3).reshape(-1, SUBLANES, LANES)


def pack_kernel(tile_hbm, id_hbm, score_hbm, out_ref, id_ref, score_ref, sems):
    tiles = tile_hbm.shape[0]
    copies = [
        pltpu.make_async_copy(id_hbm, id_ref, sems.at[0]),
        pltpu.make_async_copy(score_hbm, score_ref, sems.at[1]),
        pltpu.make_async_copy(tile_hbm, out_ref.at[pl.ds(0, tiles)], sems.at[2]),
    ]
    for copy in copies:
        copy.start()
    out_ref[tiles] = jnp.zeros((SUBLANES, LANES), jnp.bfloat16)
    out_ref[tiles + 1] = jnp.zeros((SUBLANES, LANES), jnp.bfloat16)
    top, count = id_ref.shape
    copies[0].wait()
    copies[1].wait()
    scores = score_ref[...]
    shares = scores / jnp.sum(scores, axis=0, keepdims=True)
    out_ref[tiles, :top, :count] = id_ref[...].astype(jnp.float32).astype(jnp.bfloat16)
    out_ref[tiles + 1, :top, :count] = shares.astype(jnp.bfloat16)
    copies[2].wait()


def pack(tokens, expert_ids, route_scores):
    tiles = tiles_of(tokens)
    count, top = expert_ids.shape
    return pl.pallas_call(
        pack_kernel,
        out_shape=pltpu.VMEM((tiles.shape[0] + 2, SUBLANES, LANES), jnp.bfloat16),
        in_specs=[ANY] * 3,
        out_specs=VMEM,
        scratch_shapes=[
            pltpu.VMEM((top, count), jnp.int32),
            pltpu.VMEM((top, count), jnp.float32),
            pltpu.SemaphoreType.DMA((3,)),
        ],
        compiler_params=pltpu.CompilerParams(vmem_limit_bytes=4 * MIB),
    )(in_hbm(tiles), in_hbm(expert_ids.T), in_hbm(route_scores.T))


def own_kernel(token_hbm, gate_hbm, up_hbm, gate_ref, up_ref, hidden_ref, rows_ref, sems):
    local_experts = gate_ref.shape[0]
    tokens = pltpu.make_async_copy(token_hbm, rows_ref, sems.at[2, 0])
    tokens.start()

    def load(member, which):
        source, target = ((gate_hbm, gate_ref), (up_hbm, up_ref))[which]
        return pltpu.make_async_copy(
            source.at[member], target.at[member], sems.at[which, member]
        )

    for member in range(local_experts):
        load(member, 0).start()
        load(member, 1).start()
    tokens.wait()

    def one_expert(member, carry):
        load(member, 0).wait()
        load(member, 1).wait()
        hidden_ref[member] = hidden_of(rows_ref[...], gate_ref[member], up_ref[member])
        return carry

    lax.fori_loop(0, local_experts, one_expert, 0)


def own_hidden(tokens, w_gate, w_up):
    local_experts, _, units = w_gate.shape
    count = tokens.shape[0]
    return pl.pallas_call(
        own_kernel,
        out_shape=[
            pltpu.VMEM(w_gate.shape, w_gate.dtype),
            pltpu.VMEM(w_up.shape, w_up.dtype),
            pltpu.VMEM((local_experts, count, units), jnp.bfloat16),
        ],
        in_specs=[ANY] * 3,
        out_specs=[VMEM] * 3,
        scratch_shapes=[
            pltpu.VMEM(tokens.shape, tokens.dtype),
            pltpu.SemaphoreType.DMA((3, local_experts)),
        ],
        compiler_params=pltpu.CompilerParams(vmem_limit_bytes=8 * MIB),
        cost_estimate=pl.CostEstimate(
            flops=4 * count * w_gate.size, bytes_accessed=4 * w_gate.size, transcendentals=0
        ),
    )(in_hbm(tokens), in_hbm(w_gate), in_hbm(w_up))


def spread_shares(packed_refs, spread_ref, count, top, held):
    first = lax.axis_index("expert") * held
    slots = spread_ref.shape[1]
    expert = lax.broadcasted_iota(jnp.int32, (slots, count), 0) + first
    for index, packed_ref in enumerate(packed_refs):
        tiles = packed_ref.shape[0] - 2
        ids = packed_ref[tiles].astype(jnp.float32).astype(jnp.int32)
        shares = packed_ref[tiles + 1].astype(jnp.float32)
        spread = jnp.zeros((slots, count), jnp.float32)
        for slot in range(top):
            named = expert == ids[slot : slot + 1, :count]
            spread += jnp.where(named, shares[slot : slot + 1, :count], 0.0)
        spread_ref[index * count : (index + 1) * count, :] = spread.T


def project_into(out_refs, total_ref, spread_ref, down_ref, hidden_at, count):
    local_experts, _, width = down_ref.shape
    for member in range(local_experts):
        weight = spread_ref[:, member : member + 1]
        for start in range(0, width, CHUNK):
            span = slice(start, min(start + CHUNK, width))
            scaled = weight * jnp.dot(
                hidden_at(member), down_ref[member, :, span], preferred_element_type=jnp.float32
            )
            if member:
                scaled = total_ref[:, span] + scaled
            if member < local_experts - 1:
                total_ref[:, span] = scaled
                continue
            for index, out_ref in enumerate(out_refs):
                part = scaled[index * count : (index + 1) * count]
                out_ref[:, span] = part.astype(out_ref.dtype)


def far_kernel(blocks, sent, top, *refs):
    packed_refs = refs[:blocks]
    gate_ref, up_ref, down_hbm = refs[blocks : blocks + 3]
    outs = refs[blocks + 3 :]
    out_refs, down_ref, near_ref = outs[:sent], outs[sent], outs[sent + 1]
    rows_ref, spread_ref, hidden_ref, total_ref, sems = outs[sent + 2 :]
    local_experts, width, units = gate_ref.shape
    count = rows_ref.shape[0] // blocks
    across = width // LANES
    tiles = packed_refs[0].shape[0] - 2

    def load(member):
        return pltpu.make_async_copy(down_hbm.at[member], down_ref.at[member], sems.at[member])

    @pl.loop(0, local_experts)
    def _(member):
        load(member).start()

    for index in range(blocks):
        for tile in range(tiles):
            row = index * count + tile // across * SUBLANES
            column = tile % across * LANES
            rows_ref[row : row + SUBLANES, column : column + LANES] = packed_refs[index][tile]
    spread_shares(packed_refs[:sent], spread_ref, count, top, local_experts)
    for member in range(local_experts):
        for start in range(0, units, CHUNK):
            span = slice(start, min(start + CHUNK, units))
            hidden = hidden_of(rows_ref[...], gate_ref[member, :, span], up_ref[member, :, span])
            hidden_ref[member, :, span] = hidden[: sent * count]
            if sent < blocks:
                near_ref[member, :, span] = hidden[sent * count :]
    for member in range(local_experts):
        load(member).wait()
    project_into(
        out_refs, total_ref, spread_ref, down_ref, lambda member: hidden_ref[member], count
    )


def far(packed, sent, gate, up, w_down, count, top):
    blocks = len(packed)
    local_experts, units, width = w_down.shape
    rows = blocks * count
    near_rows = max(rows - sent * count, SUBLANES)
    *parts, down, near_hidden = pl.pallas_call(
        functools.partial(far_kernel, blocks, sent, top),
        out_shape=[jax.ShapeDtypeStruct((count, width), jnp.bfloat16)] * sent
        + [
            pltpu.VMEM(w_down.shape, w_down.dtype),
            pltpu.VMEM((local_experts, near_rows, units), jnp.bfloat16),
        ],
        in_specs=[VMEM] * (blocks + 2) + [ANY],
        out_specs=[VMEM] * (sent + 2),
        scratch_shapes=[
            pltpu.VMEM((rows, width), jnp.bfloat16),
            pltpu.VMEM((sent * count, slots_of(local_experts)), jnp.float32),
            pltpu.VMEM((local_experts, sent * count, units), jnp.bfloat16),
            pltpu.VMEM((sent * count, width), jnp.float32),
            pltpu.SemaphoreType.DMA((local_experts,)),
        ],
        compiler_params=pltpu.CompilerParams(vmem_limit_bytes=12 * MIB),
        cost_estimate=pl.CostEstimate(
            flops=6 * rows * w_down.size, bytes_accessed=2 * w_down.size, transcendentals=0
        ),
    )(*packed, gate, up, in_hbm(w_down))
    return parts, down, near_hidden


def near_kernel(top, *refs):
    packed_refs, hidden_refs, down_ref = refs[:2], refs[2:4], refs[4]
    out_refs = refs[5:7]
    spread_ref, hidden_ref, total_ref = refs[7:]
    count = hidden_refs[0].shape[1]
    spread_shares(packed_refs, spread_ref, count, top, down_ref.shape[0])
    hidden_ref[:, :count, :] = hidden_refs[0][...]
    hidden_ref[:, count:, :] = hidden_refs[1][...]
    project_into(
        out_refs, total_ref, spread_ref, down_ref, lambda member: hidden_ref[member], count
    )


def near(packed, hiddens, down, top):
    local_experts, count, units = hiddens[0].shape
    width = down.shape[2]
    return pl.pallas_call(
        functools.partial(near_kernel, top),
        out_shape=[
            jax.ShapeDtypeStruct((count, width), jnp.float32),
            jax.ShapeDtypeStruct((count, width), jnp.bfloat16),
        ],
        in_specs=[VMEM] * 5,
        out_specs=[VMEM] * 2,
        scratch_shapes=[
            pltpu.VMEM((2 * count, slots_of(local_experts)), jnp.float32),
            pltpu.VMEM((local_experts, 2 * count, units), jnp.bfloat16),
            pltpu.VMEM((2 * count, width), jnp.float32),
        ],
        compiler_params=pltpu.CompilerParams(vmem_limit_bytes=8 * MIB),
        cost_estimate=pl.CostEstimate(
            flops=4 * count * down.size, bytes_accessed=2 * down.size, transcendentals=0
        ),
    )(*packed, *hiddens, down)


def exchange(array, pairs):
    return lax.ppermute(array, "expert", pairs)


def per_device(tokens, expert_ids, route_scores, w_gate, w_up, w_down):
    peers = lax.axis_size("expert")
    count, top = expert_ids.shape
    packed = pack(tokens, expert_ids, route_scores)
    if peers == 4:
        pairs = {shift: [(i, i ^ shift) for i in range(peers)] for shift in (2, 3, 1)}
        got = {s: exchange(packed, pairs[s]) for s in pairs}
        gate, up, own = own_hidden(tokens, w_gate, w_up)
        parts, down, beside = far([got[2], got[3], got[1]], 2, gate, up, w_down, count, top)
        back = [exchange(part, pairs[s]) for part, s in zip(parts, (2, 3))]
        total, part = near([packed, got[1]], [own, beside], down, top)
        back.append(exchange(part, pairs[1]))
        for part in back:
            total = total + part.astype(jnp.float32)
        return total.astype(jnp.bfloat16)
    got = lax.all_gather(packed, "expert")
    gate, up, _ = own_hidden(tokens, w_gate, w_up)
    parts = []
    for start in range(0, peers, GROUP):
        here = [got[i] for i in range(start, min(start + GROUP, peers))]
        parts += far(here, len(here), gate, up, w_down, count, top)[0]
    back = lax.all_to_all(jnp.stack(parts), "expert", 0, 0, tiled=True)
    return jnp.sum(back.astype(jnp.float32), axis=0).astype(jnp.bfloat16)


def solution(mesh):
    split = P(("groups", "expert", "dp"), None)
    held = P("expert", None, None)
    return jax.shard_map(
        per_device,
        mesh=mesh,
        in_specs=(split, split, split, held, held, held),
        out_specs=split,
        check_vma=False,
    )
```

```python
import functools

import jax
import jax.numpy as jnp
from jax import lax
from jax.experimental import pallas as pl
from jax.experimental.pallas import tpu as pltpu
from jax.sharding import PartitionSpec as P


SUBLANES, LANES = 8, 128
CHUNK = 256
GROUP = 4
MIB = 1 << 20
VMEM = pl.BlockSpec(memory_space=pltpu.VMEM)
ANY = pl.BlockSpec(memory_space=pl.ANY)


def slots_of(experts):
    return -(-experts // SUBLANES) * SUBLANES


def in_hbm(array):
    return pltpu.with_memory_space_constraint(array, pltpu.HBM)


def hidden_of(rows, gate_matrix, up_matrix):
    gate = jnp.dot(rows, gate_matrix, preferred_element_type=jnp.float32)
    up = jnp.dot(rows, up_matrix, preferred_element_type=jnp.float32)
    return (gate / (1.0 + jnp.exp(-gate)) * up).astype(jnp.bfloat16)


def tiles_of(array):
    rows, width = array.shape
    split = array.reshape(rows // SUBLANES, SUBLANES, width // LANES, LANES)
    return split.transpose(0, 2, 1, 3).reshape(-1, SUBLANES, LANES)


def pack_kernel(tile_hbm, id_hbm, score_hbm, out_ref, id_ref, score_ref, sems):
    tiles = tile_hbm.shape[0]
    copies = [
        pltpu.make_async_copy(id_hbm, id_ref, sems.at[0]),
        pltpu.make_async_copy(score_hbm, score_ref, sems.at[1]),
        pltpu.make_async_copy(tile_hbm, out_ref.at[pl.ds(0, tiles)], sems.at[2]),
    ]
    for copy in copies:
        copy.start()
    out_ref[tiles] = jnp.zeros((SUBLANES, LANES), jnp.bfloat16)
    out_ref[tiles + 1] = jnp.zeros((SUBLANES, LANES), jnp.bfloat16)
    top, count = id_ref.shape
    copies[0].wait()
    copies[1].wait()
    scores = score_ref[...]
    shares = scores / jnp.sum(scores, axis=0, keepdims=True)
    out_ref[tiles, :top, :count] = id_ref[...].astype(jnp.float32).astype(jnp.bfloat16)
    out_ref[tiles + 1, :top, :count] = shares.astype(jnp.bfloat16)
    copies[2].wait()


def pack(tokens, expert_ids, route_scores):
    tiles = tiles_of(tokens)
    count, top = expert_ids.shape
    return pl.pallas_call(
        pack_kernel,
        out_shape=pltpu.VMEM((tiles.shape[0] + 2, SUBLANES, LANES), jnp.bfloat16),
        in_specs=[ANY] * 3,
        out_specs=VMEM,
        scratch_shapes=[
            pltpu.VMEM((top, count), jnp.int32),
            pltpu.VMEM((top, count), jnp.float32),
            pltpu.SemaphoreType.DMA((3,)),
        ],
        compiler_params=pltpu.CompilerParams(vmem_limit_bytes=4 * MIB),
    )(in_hbm(tiles), in_hbm(expert_ids.T), in_hbm(route_scores.T))


def own_kernel(token_hbm, gate_hbm, up_hbm, gate_ref, up_ref, hidden_ref, rows_ref, sems):
    local_experts = gate_ref.shape[0]
    tokens = pltpu.make_async_copy(token_hbm, rows_ref, sems.at[2, 0])
    tokens.start()

    def load(member, which):
        source, target = ((gate_hbm, gate_ref), (up_hbm, up_ref))[which]
        return pltpu.make_async_copy(
            source.at[member], target.at[member], sems.at[which, member]
        )

    for member in range(local_experts):
        load(member, 0).start()
        load(member, 1).start()
    tokens.wait()

    def one_expert(member, carry):
        load(member, 0).wait()
        load(member, 1).wait()
        hidden_ref[member] = hidden_of(rows_ref[...], gate_ref[member], up_ref[member])
        return carry

    lax.fori_loop(0, local_experts, one_expert, 0)


def own_hidden(tokens, w_gate, w_up):
    local_experts, _, units = w_gate.shape
    count = tokens.shape[0]
    return pl.pallas_call(
        own_kernel,
        out_shape=[
            pltpu.VMEM(w_gate.shape, w_gate.dtype),
            pltpu.VMEM(w_up.shape, w_up.dtype),
            pltpu.VMEM((local_experts, count, units), jnp.bfloat16),
        ],
        in_specs=[ANY] * 3,
        out_specs=[VMEM] * 3,
        scratch_shapes=[
            pltpu.VMEM(tokens.shape, tokens.dtype),
            pltpu.SemaphoreType.DMA((3, local_experts)),
        ],
        compiler_params=pltpu.CompilerParams(vmem_limit_bytes=8 * MIB),
        cost_estimate=pl.CostEstimate(
            flops=4 * count * w_gate.size, bytes_accessed=4 * w_gate.size, transcendentals=0
        ),
    )(in_hbm(tokens), in_hbm(w_gate), in_hbm(w_up))


def spread_shares(packed_refs, spread_ref, count, top, held):
    first = lax.axis_index("expert") * held
    slots = spread_ref.shape[1]
    expert = lax.broadcasted_iota(jnp.int32, (slots, count), 0) + first
    for index, packed_ref in enumerate(packed_refs):
        tiles = packed_ref.shape[0] - 2
        ids = packed_ref[tiles].astype(jnp.float32).astype(jnp.int32)
        shares = packed_ref[tiles + 1].astype(jnp.float32)
        spread = jnp.zeros((slots, count), jnp.float32)
        for slot in range(top):
            named = expert == ids[slot : slot + 1, :count]
            spread += jnp.where(named, shares[slot : slot + 1, :count], 0.0)
        spread_ref[index * count : (index + 1) * count, :] = spread.T


def project_into(out_refs, total_ref, spread_ref, down_ref, hidden_at, count):
    local_experts, _, width = down_ref.shape
    for member in range(local_experts):
        weight = spread_ref[:, member : member + 1]
        for start in range(0, width, CHUNK):
            span = slice(start, min(start + CHUNK, width))
            scaled = weight * jnp.dot(
                hidden_at(member), down_ref[member, :, span], preferred_element_type=jnp.float32
            )
            if member:
                scaled = total_ref[:, span] + scaled
            if member < local_experts - 1:
                total_ref[:, span] = scaled
                continue
            for index, out_ref in enumerate(out_refs):
                part = scaled[index * count : (index + 1) * count]
                out_ref[:, span] = part.astype(out_ref.dtype)


def far_kernel(blocks, sent, top, *refs):
    packed_refs = refs[:blocks]
    gate_ref, up_ref, down_hbm = refs[blocks : blocks + 3]
    outs = refs[blocks + 3 :]
    out_refs, down_ref, near_ref = outs[:sent], outs[sent], outs[sent + 1]
    rows_ref, spread_ref, hidden_ref, total_ref, sems = outs[sent + 2 :]
    local_experts, width, units = gate_ref.shape
    count = rows_ref.shape[0] // blocks
    across = width // LANES
    tiles = packed_refs[0].shape[0] - 2

    def load(member):
        return pltpu.make_async_copy(down_hbm.at[member], down_ref.at[member], sems.at[member])

    @pl.loop(0, local_experts)
    def _(member):
        load(member).start()

    for index in range(blocks):
        for tile in range(tiles):
            row = index * count + tile // across * SUBLANES
            column = tile % across * LANES
            rows_ref[row : row + SUBLANES, column : column + LANES] = packed_refs[index][tile]
    spread_shares(packed_refs[:sent], spread_ref, count, top, local_experts)
    for member in range(local_experts):
        for start in range(0, units, CHUNK):
            span = slice(start, min(start + CHUNK, units))
            hidden = hidden_of(rows_ref[...], gate_ref[member, :, span], up_ref[member, :, span])
            hidden_ref[member, :, span] = hidden[: sent * count]
            if sent < blocks:
                near_ref[member, :, span] = hidden[sent * count :]
    for member in range(local_experts):
        load(member).wait()
    project_into(
        out_refs, total_ref, spread_ref, down_ref, lambda member: hidden_ref[member], count
    )


def far(packed, sent, gate, up, w_down, count, top):
    blocks = len(packed)
    local_experts, units, width = w_down.shape
    rows = blocks * count
    near_rows = max(rows - sent * count, SUBLANES)
    *parts, down, near_hidden = pl.pallas_call(
        functools.partial(far_kernel, blocks, sent, top),
        out_shape=[jax.ShapeDtypeStruct((count, width), jnp.bfloat16)] * sent
        + [
            pltpu.VMEM(w_down.shape, w_down.dtype),
            pltpu.VMEM((local_experts, near_rows, units), jnp.bfloat16),
        ],
        in_specs=[VMEM] * (blocks + 2) + [ANY],
        out_specs=[VMEM] * (sent + 2),
        scratch_shapes=[
            pltpu.VMEM((rows, width), jnp.bfloat16),
            pltpu.VMEM((sent * count, slots_of(local_experts)), jnp.float32),
            pltpu.VMEM((local_experts, sent * count, units), jnp.bfloat16),
            pltpu.VMEM((sent * count, width), jnp.float32),
            pltpu.SemaphoreType.DMA((local_experts,)),
        ],
        compiler_params=pltpu.CompilerParams(vmem_limit_bytes=12 * MIB),
        cost_estimate=pl.CostEstimate(
            flops=6 * rows * w_down.size, bytes_accessed=2 * w_down.size, transcendentals=0
        ),
    )(*packed, gate, up, in_hbm(w_down))
    return parts, down, near_hidden


def near_kernel(top, *refs):
    packed_refs, hidden_refs, down_ref = refs[:2], refs[2:4], refs[4]
    out_refs = refs[5:7]
    spread_ref, hidden_ref, total_ref = refs[7:]
    count = hidden_refs[0].shape[1]
    spread_shares(packed_refs, spread_ref, count, top, down_ref.shape[0])
    hidden_ref[:, :count, :] = hidden_refs[0][...]
    hidden_ref[:, count:, :] = hidden_refs[1][...]
    project_into(
        out_refs, total_ref, spread_ref, down_ref, lambda member: hidden_ref[member], count
    )


def near(packed, hiddens, down, top):
    local_experts, count, units = hiddens[0].shape
    width = down.shape[2]
    return pl.pallas_call(
        functools.partial(near_kernel, top),
        out_shape=[
            jax.ShapeDtypeStruct((count, width), jnp.float32),
            jax.ShapeDtypeStruct((count, width), jnp.bfloat16),
        ],
        in_specs=[VMEM] * 5,
        out_specs=[VMEM] * 2,
        scratch_shapes=[
            pltpu.VMEM((2 * count, slots_of(local_experts)), jnp.float32),
            pltpu.VMEM((local_experts, 2 * count, units), jnp.bfloat16),
            pltpu.VMEM((2 * count, width), jnp.float32),
        ],
        compiler_params=pltpu.CompilerParams(vmem_limit_bytes=8 * MIB),
        cost_estimate=pl.CostEstimate(
            flops=4 * count * down.size, bytes_accessed=2 * down.size, transcendentals=0
        ),
    )(*packed, *hiddens, down)


def exchange(array, pairs):
    return lax.ppermute(array, "expert", pairs)


def per_device(tokens, expert_ids, route_scores, w_gate, w_up, w_down):
    peers = lax.axis_size("expert")
    count, top = expert_ids.shape
    packed = pack(tokens, expert_ids, route_scores)
    if peers == 4:
        pairs = {shift: [(i, i ^ shift) for i in range(peers)] for shift in (2, 3, 1)}
        got = {s: exchange(packed, pairs[s]) for s in pairs}
        gate, up, own = own_hidden(tokens, w_gate, w_up)
        parts, down, beside = far([got[2], got[3], got[1]], 2, gate, up, w_down, count, top)
        back = [
            exchange(parts[1], pairs[3][1:3]),
            exchange(parts[0], pairs[2]),
            exchange(parts[1], pairs[3][::3]),
        ]
        total, part = near([packed, got[1]], [own, beside], down, top)
        back.append(exchange(part, pairs[1]))
        for part in back:
            total = total + part.astype(jnp.float32)
        return total.astype(jnp.bfloat16)
    got = lax.all_gather(packed, "expert")
    gate, up, _ = own_hidden(tokens, w_gate, w_up)
    parts = []
    for start in range(0, peers, GROUP):
        here = [got[i] for i in range(start, min(start + GROUP, peers))]
        parts += far(here, len(here), gate, up, w_down, count, top)[0]
    back = lax.all_to_all(jnp.stack(parts), "expert", 0, 0, tiled=True)
    return jnp.sum(back.astype(jnp.float32), axis=0).astype(jnp.bfloat16)


def solution(mesh):
    split = P(("groups", "expert", "dp"), None)
    held = P("expert", None, None)
    return jax.shard_map(
        per_device,
        mesh=mesh,
        in_specs=(split, split, split, held, held, held),
        out_specs=split,
        check_vma=False,
    )
```

```python
import functools

import jax
import jax.numpy as jnp
from jax import lax
from jax.experimental import pallas as pl
from jax.experimental.pallas import tpu as pltpu
from jax.sharding import PartitionSpec as P


SUBLANES, LANES = 8, 128
CHUNK = 256
GROUP = 4
MIB = 1 << 20
VMEM = pl.BlockSpec(memory_space=pltpu.VMEM)
ANY = pl.BlockSpec(memory_space=pl.ANY)


def slots_of(experts):
    return -(-experts // SUBLANES) * SUBLANES


def in_hbm(array):
    return pltpu.with_memory_space_constraint(array, pltpu.HBM)


def hidden_of(rows, gate_matrix, up_matrix):
    gate = jnp.dot(rows, gate_matrix, preferred_element_type=jnp.float32)
    up = jnp.dot(rows, up_matrix, preferred_element_type=jnp.float32)
    return (gate / (1.0 + jnp.exp(-gate)) * up).astype(jnp.bfloat16)


def tiles_of(array):
    rows, width = array.shape
    split = array.reshape(rows // SUBLANES, SUBLANES, width // LANES, LANES)
    return split.transpose(0, 2, 1, 3).reshape(-1, SUBLANES, LANES)


def pack_kernel(tile_hbm, id_hbm, score_hbm, out_ref, id_ref, score_ref, sems):
    tiles = tile_hbm.shape[0]
    copies = [
        pltpu.make_async_copy(id_hbm, id_ref, sems.at[0]),
        pltpu.make_async_copy(score_hbm, score_ref, sems.at[1]),
        pltpu.make_async_copy(tile_hbm, out_ref.at[pl.ds(0, tiles)], sems.at[2]),
    ]
    for copy in copies:
        copy.start()
    out_ref[tiles] = jnp.zeros((SUBLANES, LANES), jnp.bfloat16)
    out_ref[tiles + 1] = jnp.zeros((SUBLANES, LANES), jnp.bfloat16)
    top, count = id_ref.shape
    copies[0].wait()
    copies[1].wait()
    scores = score_ref[...]
    shares = scores / jnp.sum(scores, axis=0, keepdims=True)
    out_ref[tiles, :top, :count] = id_ref[...].astype(jnp.float32).astype(jnp.bfloat16)
    out_ref[tiles + 1, :top, :count] = shares.astype(jnp.bfloat16)
    copies[2].wait()


def pack(tokens, expert_ids, route_scores):
    tiles = tiles_of(tokens)
    count, top = expert_ids.shape
    return pl.pallas_call(
        pack_kernel,
        out_shape=pltpu.VMEM((tiles.shape[0] + 2, SUBLANES, LANES), jnp.bfloat16),
        in_specs=[ANY] * 3,
        out_specs=VMEM,
        scratch_shapes=[
            pltpu.VMEM((top, count), jnp.int32),
            pltpu.VMEM((top, count), jnp.float32),
            pltpu.SemaphoreType.DMA((3,)),
        ],
        compiler_params=pltpu.CompilerParams(vmem_limit_bytes=4 * MIB),
    )(in_hbm(tiles), in_hbm(expert_ids.T), in_hbm(route_scores.T))


def own_kernel(token_hbm, gate_hbm, up_hbm, gate_ref, up_ref, hidden_ref, rows_ref, sems):
    local_experts = gate_ref.shape[0]
    tokens = pltpu.make_async_copy(token_hbm, rows_ref, sems.at[2, 0])
    tokens.start()

    def load(member, which):
        source, target = ((gate_hbm, gate_ref), (up_hbm, up_ref))[which]
        return pltpu.make_async_copy(
            source.at[member], target.at[member], sems.at[which, member]
        )

    for member in range(local_experts):
        load(member, 0).start()
        load(member, 1).start()
    tokens.wait()

    def one_expert(member, carry):
        load(member, 0).wait()
        load(member, 1).wait()
        hidden_ref[member] = hidden_of(rows_ref[...], gate_ref[member], up_ref[member])
        return carry

    lax.fori_loop(0, local_experts, one_expert, 0)


def own_hidden(tokens, w_gate, w_up):
    local_experts, _, units = w_gate.shape
    count = tokens.shape[0]
    return pl.pallas_call(
        own_kernel,
        out_shape=[
            pltpu.VMEM(w_gate.shape, w_gate.dtype),
            pltpu.VMEM(w_up.shape, w_up.dtype),
            pltpu.VMEM((local_experts, count, units), jnp.bfloat16),
        ],
        in_specs=[ANY] * 3,
        out_specs=[VMEM] * 3,
        scratch_shapes=[
            pltpu.VMEM(tokens.shape, tokens.dtype),
            pltpu.SemaphoreType.DMA((3, local_experts)),
        ],
        compiler_params=pltpu.CompilerParams(vmem_limit_bytes=8 * MIB),
        cost_estimate=pl.CostEstimate(
            flops=4 * count * w_gate.size, bytes_accessed=4 * w_gate.size, transcendentals=0
        ),
    )(in_hbm(tokens), in_hbm(w_gate), in_hbm(w_up))


def spread_shares(packed_refs, spread_ref, count, top, held):
    first = lax.axis_index("expert") * held
    slots = spread_ref.shape[1]
    expert = lax.broadcasted_iota(jnp.int32, (slots, count), 0) + first
    for index, packed_ref in enumerate(packed_refs):
        tiles = packed_ref.shape[0] - 2
        ids = packed_ref[tiles].astype(jnp.float32).astype(jnp.int32)
        shares = packed_ref[tiles + 1].astype(jnp.float32)
        spread = jnp.zeros((slots, count), jnp.float32)
        for slot in range(top):
            named = expert == ids[slot : slot + 1, :count]
            spread += jnp.where(named, shares[slot : slot + 1, :count], 0.0)
        spread_ref[index * count : (index + 1) * count, :] = spread.T


def project_into(out_refs, total_ref, spread_ref, down_ref, hidden_at, count):
    local_experts, _, width = down_ref.shape
    for member in range(local_experts):
        weight = spread_ref[:, member : member + 1]
        for start in range(0, width, CHUNK):
            span = slice(start, min(start + CHUNK, width))
            scaled = weight * jnp.dot(
                hidden_at(member), down_ref[member, :, span], preferred_element_type=jnp.float32
            )
            if member:
                scaled = total_ref[:, span] + scaled
            if member < local_experts - 1:
                total_ref[:, span] = scaled
                continue
            for index, out_ref in enumerate(out_refs):
                part = scaled[index * count : (index + 1) * count]
                out_ref[:, span] = part.astype(out_ref.dtype)


def far_kernel(blocks, sent, top, *refs):
    packed_refs = refs[:blocks]
    gate_ref, up_ref, down_hbm = refs[blocks : blocks + 3]
    outs = refs[blocks + 3 :]
    out_refs, down_ref, near_ref = outs[:sent], outs[sent], outs[sent + 1]
    rows_ref, spread_ref, hidden_ref, total_ref, sems = outs[sent + 2 :]
    local_experts, width, units = gate_ref.shape
    count = rows_ref.shape[0] // blocks
    across = width // LANES
    tiles = packed_refs[0].shape[0] - 2

    def load(member):
        return pltpu.make_async_copy(down_hbm.at[member], down_ref.at[member], sems.at[member])

    @pl.loop(0, local_experts)
    def _(member):
        load(member).start()

    for index in range(blocks):
        for tile in range(tiles):
            row = index * count + tile // across * SUBLANES
            column = tile % across * LANES
            rows_ref[row : row + SUBLANES, column : column + LANES] = packed_refs[index][tile]
    spread_shares(packed_refs[:sent], spread_ref, count, top, local_experts)
    for member in range(local_experts):
        for start in range(0, units, CHUNK):
            span = slice(start, min(start + CHUNK, units))
            hidden = hidden_of(rows_ref[...], gate_ref[member, :, span], up_ref[member, :, span])
            hidden_ref[member, :, span] = hidden[: sent * count]
            if sent < blocks:
                near_ref[member, :, span] = hidden[sent * count :]
    for member in range(local_experts):
        load(member).wait()
    project_into(
        out_refs, total_ref, spread_ref, down_ref, lambda member: hidden_ref[member], count
    )


def far(packed, sent, gate, up, w_down, count, top):
    blocks = len(packed)
    local_experts, units, width = w_down.shape
    rows = blocks * count
    near_rows = max(rows - sent * count, SUBLANES)
    *parts, down, near_hidden = pl.pallas_call(
        functools.partial(far_kernel, blocks, sent, top),
        out_shape=[jax.ShapeDtypeStruct((count, width), jnp.bfloat16)] * sent
        + [
            pltpu.VMEM(w_down.shape, w_down.dtype),
            pltpu.VMEM((local_experts, near_rows, units), jnp.bfloat16),
        ],
        in_specs=[VMEM] * (blocks + 2) + [ANY],
        out_specs=[VMEM] * (sent + 2),
        scratch_shapes=[
            pltpu.VMEM((rows, width), jnp.bfloat16),
            pltpu.VMEM((sent * count, slots_of(local_experts)), jnp.float32),
            pltpu.VMEM((local_experts, sent * count, units), jnp.bfloat16),
            pltpu.VMEM((sent * count, width), jnp.float32),
            pltpu.SemaphoreType.DMA((local_experts,)),
        ],
        compiler_params=pltpu.CompilerParams(vmem_limit_bytes=12 * MIB),
        cost_estimate=pl.CostEstimate(
            flops=6 * rows * w_down.size, bytes_accessed=2 * w_down.size, transcendentals=0
        ),
    )(*packed, gate, up, in_hbm(w_down))
    return parts, down, near_hidden


def near_kernel(blocks, top, *refs):
    packed_refs, hidden_refs = refs[:blocks], refs[blocks : blocks + 2]
    down_ref = refs[blocks + 2]
    out_refs = refs[blocks + 3 : 2 * blocks + 3]
    spread_ref, hidden_ref, total_ref = refs[2 * blocks + 3 :]
    count = hidden_refs[0].shape[1]
    spread_shares(packed_refs, spread_ref, count, top, down_ref.shape[0])
    hidden_ref[:, :count, :] = hidden_refs[0][...]
    hidden_ref[:, count:, :] = hidden_refs[1][...]
    project_into(
        out_refs, total_ref, spread_ref, down_ref, lambda member: hidden_ref[member], count
    )


def near(packed, hiddens, down, kinds, top):
    blocks = len(packed)
    local_experts, count, units = hiddens[0].shape
    width = down.shape[2]
    rows = blocks * count
    return pl.pallas_call(
        functools.partial(near_kernel, blocks, top),
        out_shape=[jax.ShapeDtypeStruct((count, width), kind) for kind in kinds],
        in_specs=[VMEM] * (blocks + 3),
        out_specs=[VMEM] * blocks,
        scratch_shapes=[
            pltpu.VMEM((rows, slots_of(local_experts)), jnp.float32),
            pltpu.VMEM((local_experts, rows, units), jnp.bfloat16),
            pltpu.VMEM((rows, width), jnp.float32),
        ],
        compiler_params=pltpu.CompilerParams(vmem_limit_bytes=10 * MIB),
        cost_estimate=pl.CostEstimate(
            flops=2 * rows * down.size, bytes_accessed=2 * down.size, transcendentals=0
        ),
    )(*packed, *hiddens, down)


def exchange(array, pairs):
    return lax.ppermute(array, "expert", pairs)


def per_device(tokens, expert_ids, route_scores, w_gate, w_up, w_down):
    peers = lax.axis_size("expert")
    count, top = expert_ids.shape
    packed = pack(tokens, expert_ids, route_scores)
    if peers == 4:
        pairs = {shift: [(i, i ^ shift) for i in range(peers)] for shift in (2, 3, 1)}
        got = {s: exchange(packed, pairs[s]) for s in pairs}
        gate, up, own = own_hidden(tokens, w_gate, w_up)
        order = [got[3], got[2], got[1]]
        parts, down, beside = far(order, 1, gate, up, w_down, count, top)
        hop = exchange(parts[0], pairs[1])
        kinds = (jnp.float32, jnp.float32, jnp.bfloat16)
        total, part, beside_part = near([packed, got[2], got[1]], [own, beside], down, kinds, top)
        both = (part + hop.astype(jnp.float32)).astype(jnp.bfloat16)
        back = [exchange(both, pairs[2]), exchange(beside_part, pairs[1])]
        for part in back:
            total = total + part.astype(jnp.float32)
        return total.astype(jnp.bfloat16)
    got = lax.all_gather(packed, "expert")
    gate, up, _ = own_hidden(tokens, w_gate, w_up)
    parts = []
    for start in range(0, peers, GROUP):
        here = [got[i] for i in range(start, min(start + GROUP, peers))]
        parts += far(here, len(here), gate, up, w_down, count, top)[0]
    back = lax.all_to_all(jnp.stack(parts), "expert", 0, 0, tiled=True)
    return jnp.sum(back.astype(jnp.float32), axis=0).astype(jnp.bfloat16)


def solution(mesh):
    split = P(("groups", "expert", "dp"), None)
    held = P("expert", None, None)
    return jax.shard_map(
        per_device,
        mesh=mesh,
        in_specs=(split, split, split, held, held, held),
        out_specs=split,
        check_vma=False,
    )
```

```python
import functools

import jax
import jax.numpy as jnp
from jax import lax
from jax.experimental import pallas as pl
from jax.experimental.pallas import tpu as pltpu
from jax.sharding import PartitionSpec as P


SUBLANES, LANES = 8, 128
CHUNK = 256
GROUP = 4
MIB = 1 << 20
VMEM = pl.BlockSpec(memory_space=pltpu.VMEM)
ANY = pl.BlockSpec(memory_space=pl.ANY)


def slots_of(experts):
    return -(-experts // SUBLANES) * SUBLANES


def in_hbm(array):
    return pltpu.with_memory_space_constraint(array, pltpu.HBM)


def hidden_of(rows, gate_matrix, up_matrix):
    gate = jnp.dot(rows, gate_matrix, preferred_element_type=jnp.float32)
    up = jnp.dot(rows, up_matrix, preferred_element_type=jnp.float32)
    return (gate / (1.0 + jnp.exp(-gate)) * up).astype(jnp.bfloat16)


def tiles_of(array):
    rows, width = array.shape
    split = array.reshape(rows // SUBLANES, SUBLANES, width // LANES, LANES)
    return split.transpose(0, 2, 1, 3).reshape(-1, SUBLANES, LANES)


def pack_kernel(tile_hbm, id_hbm, score_hbm, out_ref, id_ref, score_ref, sems):
    tiles = tile_hbm.shape[0]
    copies = [
        pltpu.make_async_copy(id_hbm, id_ref, sems.at[0]),
        pltpu.make_async_copy(score_hbm, score_ref, sems.at[1]),
        pltpu.make_async_copy(tile_hbm, out_ref.at[pl.ds(0, tiles)], sems.at[2]),
    ]
    for copy in copies:
        copy.start()
    out_ref[tiles] = jnp.zeros((SUBLANES, LANES), jnp.bfloat16)
    out_ref[tiles + 1] = jnp.zeros((SUBLANES, LANES), jnp.bfloat16)
    top, count = id_ref.shape
    copies[0].wait()
    copies[1].wait()
    scores = score_ref[...]
    shares = scores / jnp.sum(scores, axis=0, keepdims=True)
    out_ref[tiles, :top, :count] = id_ref[...].astype(jnp.float32).astype(jnp.bfloat16)
    out_ref[tiles + 1, :top, :count] = shares.astype(jnp.bfloat16)
    copies[2].wait()


def pack(tokens, expert_ids, route_scores):
    tiles = tiles_of(tokens)
    count, top = expert_ids.shape
    return pl.pallas_call(
        pack_kernel,
        out_shape=pltpu.VMEM((tiles.shape[0] + 2, SUBLANES, LANES), jnp.bfloat16),
        in_specs=[ANY] * 3,
        out_specs=VMEM,
        scratch_shapes=[
            pltpu.VMEM((top, count), jnp.int32),
            pltpu.VMEM((top, count), jnp.float32),
            pltpu.SemaphoreType.DMA((3,)),
        ],
        compiler_params=pltpu.CompilerParams(vmem_limit_bytes=4 * MIB),
    )(in_hbm(tiles), in_hbm(expert_ids.T), in_hbm(route_scores.T))


def own_kernel(begin, token_hbm, gate_hbm, up_hbm, gate_ref, up_ref, hidden_ref, rows_ref, sems):
    local_experts = gate_ref.shape[0]
    tokens = pltpu.make_async_copy(token_hbm, rows_ref, sems.at[2, 0])
    tokens.start()

    def load(member, which):
        source, target = ((gate_hbm, gate_ref), (up_hbm, up_ref))[which]
        return pltpu.make_async_copy(
            source.at[begin + member], target.at[member], sems.at[which, member]
        )

    for member in range(local_experts):
        load(member, 0).start()
        load(member, 1).start()
    tokens.wait()

    def one_expert(member, carry):
        load(member, 0).wait()
        load(member, 1).wait()
        hidden_ref[member] = hidden_of(rows_ref[...], gate_ref[member], up_ref[member])
        return carry

    lax.fori_loop(0, local_experts, one_expert, 0)


def own_hidden(tokens, w_gate, w_up, begin, end):
    _, width, units = w_gate.shape
    held = end - begin
    count = tokens.shape[0]
    return pl.pallas_call(
        functools.partial(own_kernel, begin),
        out_shape=[
            pltpu.VMEM((held, width, units), w_gate.dtype),
            pltpu.VMEM((held, width, units), w_up.dtype),
            pltpu.VMEM((held, count, units), jnp.bfloat16),
        ],
        in_specs=[ANY] * 3,
        out_specs=[VMEM] * 3,
        scratch_shapes=[
            pltpu.VMEM(tokens.shape, tokens.dtype),
            pltpu.SemaphoreType.DMA((3, held)),
        ],
        compiler_params=pltpu.CompilerParams(vmem_limit_bytes=8 * MIB),
        cost_estimate=pl.CostEstimate(
            flops=4 * count * held * width * units,
            bytes_accessed=4 * held * width * units,
            transcendentals=0,
        ),
    )(in_hbm(tokens), in_hbm(w_gate), in_hbm(w_up))


def spread_shares(packed_refs, spread_ref, count, top, held):
    first = lax.axis_index("expert") * held
    slots = spread_ref.shape[1]
    expert = lax.broadcasted_iota(jnp.int32, (slots, count), 0) + first
    for index, packed_ref in enumerate(packed_refs):
        tiles = packed_ref.shape[0] - 2
        ids = packed_ref[tiles].astype(jnp.float32).astype(jnp.int32)
        shares = packed_ref[tiles + 1].astype(jnp.float32)
        spread = jnp.zeros((slots, count), jnp.float32)
        for slot in range(top):
            named = expert == ids[slot : slot + 1, :count]
            spread += jnp.where(named, shares[slot : slot + 1, :count], 0.0)
        spread_ref[index * count : (index + 1) * count, :] = spread.T


def project_into(out_refs, total_ref, spread_ref, down_ref, hidden_at, count, before=None):
    local_experts, _, width = down_ref.shape
    for member in range(local_experts):
        if before is not None:
            before(member)
        weight = spread_ref[:, member : member + 1]
        for start in range(0, width, CHUNK):
            span = slice(start, min(start + CHUNK, width))
            scaled = weight * jnp.dot(
                hidden_at(member), down_ref[member, :, span], preferred_element_type=jnp.float32
            )
            if member:
                scaled = total_ref[:, span] + scaled
            if member < local_experts - 1:
                total_ref[:, span] = scaled
                continue
            for index, out_ref in enumerate(out_refs):
                part = scaled[index * count : (index + 1) * count]
                out_ref[:, span] = part.astype(out_ref.dtype)


def far_kernel(blocks, sent, pieces, late, top, *refs):
    packed_refs, refs = refs[:blocks], refs[blocks:]
    gate_refs, up_refs, refs = refs[:pieces], refs[pieces : 2 * pieces], refs[2 * pieces :]
    gate_hbm, up_hbm, down_hbm, *refs = refs
    out_refs, refs = refs[:sent], refs[sent:]
    down_ref, near_ref, own_ref, *refs = refs
    rows_ref, spread_ref, hidden_ref, total_ref, late_ref, sems, late_sems = refs
    local_experts, _, width = down_ref.shape
    units = down_ref.shape[1]
    count = own_ref.shape[1]
    received = blocks - 1 if late else blocks
    across = width // LANES
    tiles = packed_refs[0].shape[0] - 2
    early = local_experts - late

    def load(member):
        return pltpu.make_async_copy(down_hbm.at[member], down_ref.at[member], sems.at[member])

    def load_late(index, which):
        source = (gate_hbm, up_hbm)[which].at[early + index]
        return pltpu.make_async_copy(
            source, late_ref.at[which, index], late_sems.at[which, index]
        )

    for index in range(late):
        load_late(index, 0).start()
        load_late(index, 1).start()

    @pl.loop(0, local_experts)
    def _(member):
        load(member).start()

    for index in range(blocks):
        for tile in range(tiles):
            row = index * count + tile // across * SUBLANES
            column = tile % across * LANES
            rows_ref[row : row + SUBLANES, column : column + LANES] = packed_refs[index][tile]
    spread_shares(packed_refs[:sent], spread_ref, count, top, local_experts)
    gates = [ref.at[index] for ref in gate_refs for index in range(ref.shape[0])]
    ups = [ref.at[index] for ref in up_refs for index in range(ref.shape[0])]
    gates += [late_ref.at[0, index] for index in range(late)]
    ups += [late_ref.at[1, index] for index in range(late)]
    for member in range(local_experts):
        rows = received * count
        if member >= early:
            load_late(member - early, 0).wait()
            load_late(member - early, 1).wait()
            rows = blocks * count
        for start in range(0, units, CHUNK):
            span = slice(start, min(start + CHUNK, units))
            hidden = hidden_of(rows_ref[:rows, :], gates[member][:, span], ups[member][:, span])
            hidden_ref[member, :, span] = hidden[: sent * count]
            if sent < received:
                near_ref[member, :, span] = hidden[sent * count : received * count]
            if member >= early:
                own_ref[member - early, :, span] = hidden[received * count :]
    half = max(local_experts // 2, 1)

    def arrived(member):
        if member % half == 0:
            for other in range(member, min(member + half, local_experts)):
                load(other).wait()

    project_into(
        out_refs,
        total_ref,
        spread_ref,
        down_ref,
        lambda member: hidden_ref[member],
        count,
        arrived,
    )


def far(packed, sent, gates, ups, weights, late, count, top):
    w_gate, w_up, w_down = weights
    blocks = len(packed)
    local_experts, units, width = w_down.shape
    rows = blocks * count
    received = blocks - 1 if late else blocks
    near_rows = max((received - sent) * count, SUBLANES)
    some = max(late, 1)
    *parts, down, near_hidden, own = pl.pallas_call(
        functools.partial(far_kernel, blocks, sent, len(gates), late, top),
        out_shape=[jax.ShapeDtypeStruct((count, width), jnp.bfloat16)] * sent
        + [
            pltpu.VMEM(w_down.shape, w_down.dtype),
            pltpu.VMEM((local_experts, near_rows, units), jnp.bfloat16),
            pltpu.VMEM((some, count, units), jnp.bfloat16),
        ],
        in_specs=[VMEM] * (blocks + 2 * len(gates)) + [ANY] * 3,
        out_specs=[VMEM] * (sent + 3),
        scratch_shapes=[
            pltpu.VMEM((rows, width), jnp.bfloat16),
            pltpu.VMEM((sent * count, slots_of(local_experts)), jnp.float32),
            pltpu.VMEM((local_experts, sent * count, units), jnp.bfloat16),
            pltpu.VMEM((sent * count, width), jnp.float32),
            pltpu.VMEM((2, some, width, units), jnp.bfloat16),
            pltpu.SemaphoreType.DMA((local_experts,)),
            pltpu.SemaphoreType.DMA((2, some)),
        ],
        compiler_params=pltpu.CompilerParams(vmem_limit_bytes=14 * MIB),
        cost_estimate=pl.CostEstimate(
            flops=6 * rows * w_down.size, bytes_accessed=2 * w_down.size, transcendentals=0
        ),
    )(*packed, *gates, *ups, in_hbm(w_gate), in_hbm(w_up), in_hbm(w_down))
    return parts, down, near_hidden, own


def near_kernel(blocks, pieces, top, *refs):
    packed_refs, refs = refs[:blocks], refs[blocks:]
    own_refs, refs = refs[:pieces], refs[pieces:]
    beside_ref, down_ref, *refs = refs
    out_refs = refs[:blocks]
    spread_ref, hidden_ref, total_ref = refs[blocks:]
    count = own_refs[0].shape[1]
    spread_shares(packed_refs, spread_ref, count, top, down_ref.shape[0])
    begin = 0
    for own_ref in own_refs:
        end = begin + own_ref.shape[0]
        hidden_ref[begin:end, :count, :] = own_ref[...]
        begin = end
    hidden_ref[:, count:, :] = beside_ref[...]
    project_into(
        out_refs, total_ref, spread_ref, down_ref, lambda member: hidden_ref[member], count
    )


def near(packed, owns, beside, down, kinds, top):
    blocks = len(packed)
    local_experts, units, width = down.shape
    count = owns[0].shape[1]
    rows = blocks * count
    return pl.pallas_call(
        functools.partial(near_kernel, blocks, len(owns), top),
        out_shape=[jax.ShapeDtypeStruct((count, width), kind) for kind in kinds],
        in_specs=[VMEM] * (blocks + len(owns) + 2),
        out_specs=[VMEM] * blocks,
        scratch_shapes=[
            pltpu.VMEM((rows, slots_of(local_experts)), jnp.float32),
            pltpu.VMEM((local_experts, rows, units), jnp.bfloat16),
            pltpu.VMEM((rows, width), jnp.float32),
        ],
        compiler_params=pltpu.CompilerParams(vmem_limit_bytes=10 * MIB),
        cost_estimate=pl.CostEstimate(
            flops=2 * rows * down.size, bytes_accessed=2 * down.size, transcendentals=0
        ),
    )(*packed, *owns, beside, down)


def exchange(array, pairs):
    return lax.ppermute(array, "expert", pairs)


def per_device(tokens, expert_ids, route_scores, w_gate, w_up, w_down):
    peers = lax.axis_size("expert")
    count, top = expert_ids.shape
    packed = pack(tokens, expert_ids, route_scores)
    weights = (w_gate, w_up, w_down)
    experts = w_gate.shape[0]
    if peers == 4 and experts >= 4:
        pairs = {shift: [(i, i ^ shift) for i in range(peers)] for shift in (2, 1)}
        got = {shift: exchange(packed, pairs[shift]) for shift in pairs}
        late = 1
        cut = experts // 2
        first = own_hidden(tokens, w_gate, w_up, 0, cut)
        got[3] = exchange(got[2], pairs[1])
        second = own_hidden(tokens, w_gate, w_up, cut, experts - late)
        gates, ups, owns = zip(first, second)
        order = [got[3], got[2], got[1], packed]
        parts, down, beside, last = far(order, 1, gates, ups, weights, late, count, top)
        hop = exchange(parts[0], pairs[1])
        kinds = (jnp.float32, jnp.float32, jnp.bfloat16)
        total, part, beside_part = near(
            [packed, got[2], got[1]], [*owns, last], beside, down, kinds, top
        )
        both = (part + hop.astype(jnp.float32)).astype(jnp.bfloat16)
        back = [exchange(both, pairs[2]), exchange(beside_part, pairs[1])]
        for part in back:
            total = total + part.astype(jnp.float32)
        return total.astype(jnp.bfloat16)
    got = lax.all_gather(packed, "expert")
    gate, up, _ = own_hidden(tokens, w_gate, w_up, 0, experts)
    parts = []
    for start in range(0, peers, GROUP):
        here = [got[i] for i in range(start, min(start + GROUP, peers))]
        parts += far(here, len(here), [gate], [up], weights, 0, count, top)[0]
    back = lax.all_to_all(jnp.stack(parts), "expert", 0, 0, tiled=True)
    return jnp.sum(back.astype(jnp.float32), axis=0).astype(jnp.bfloat16)


def solution(mesh):
    split = P(("groups", "expert", "dp"), None)
    held = P("expert", None, None)
    return jax.shard_map(
        per_device,
        mesh=mesh,
        in_specs=(split, split, split, held, held, held),
        out_specs=split,
        check_vma=False,
    )
```

```python
import functools

import jax
import jax.numpy as jnp
from jax import lax
from jax.experimental import pallas as pl
from jax.experimental.pallas import tpu as pltpu
from jax.sharding import PartitionSpec as P


SUBLANES, LANES = 8, 128
CHUNK = 256
PIECES = 4
GROUP = 4
MIB = 1 << 20
VMEM = pl.BlockSpec(memory_space=pltpu.VMEM)
ANY = pl.BlockSpec(memory_space=pl.ANY)


def slots_of(experts):
    return -(-experts // SUBLANES) * SUBLANES


def in_hbm(array):
    return pltpu.with_memory_space_constraint(array, pltpu.HBM)


def hidden_of(rows, gate_matrix, up_matrix):
    gate = jnp.dot(rows, gate_matrix, preferred_element_type=jnp.float32)
    up = jnp.dot(rows, up_matrix, preferred_element_type=jnp.float32)
    return (gate / (1.0 + jnp.exp(-gate)) * up).astype(jnp.bfloat16)


def tiles_of(array):
    rows, width = array.shape
    split = array.reshape(rows // SUBLANES, SUBLANES, width // LANES, LANES)
    return split.transpose(0, 2, 1, 3).reshape(-1, SUBLANES, LANES)


def pack_kernel(tile_hbm, id_hbm, score_hbm, out_ref, id_ref, score_ref, sems):
    tiles = tile_hbm.shape[0]
    copies = [
        pltpu.make_async_copy(id_hbm, id_ref, sems.at[0]),
        pltpu.make_async_copy(score_hbm, score_ref, sems.at[1]),
    ]
    piece = -(-tiles // PIECES)
    for index, begin in enumerate(range(0, tiles, piece)):
        span = pl.ds(begin, min(piece, tiles - begin))
        copies.append(
            pltpu.make_async_copy(tile_hbm.at[span], out_ref.at[span], sems.at[2 + index])
        )
    for copy in copies:
        copy.start()
    out_ref[tiles] = jnp.zeros((SUBLANES, LANES), jnp.bfloat16)
    out_ref[tiles + 1] = jnp.zeros((SUBLANES, LANES), jnp.bfloat16)
    top, count = id_ref.shape
    copies[0].wait()
    copies[1].wait()
    scores = score_ref[...]
    shares = scores / jnp.sum(scores, axis=0, keepdims=True)
    out_ref[tiles, :top, :count] = id_ref[...].astype(jnp.float32).astype(jnp.bfloat16)
    out_ref[tiles + 1, :top, :count] = shares.astype(jnp.bfloat16)
    for copy in copies[2:]:
        copy.wait()


def pack(tokens, expert_ids, route_scores):
    tiles = tiles_of(tokens)
    count, top = expert_ids.shape
    return pl.pallas_call(
        pack_kernel,
        out_shape=pltpu.VMEM((tiles.shape[0] + 2, SUBLANES, LANES), jnp.bfloat16),
        in_specs=[ANY] * 3,
        out_specs=VMEM,
        scratch_shapes=[
            pltpu.VMEM((top, count), jnp.int32),
            pltpu.VMEM((top, count), jnp.float32),
            pltpu.SemaphoreType.DMA((2 + PIECES,)),
        ],
        compiler_params=pltpu.CompilerParams(vmem_limit_bytes=4 * MIB),
    )(in_hbm(tiles), in_hbm(expert_ids.T), in_hbm(route_scores.T))


def own_kernel(token_hbm, gate_hbm, up_hbm, gate_ref, up_ref, hidden_ref, rows_ref, sems):
    local_experts = gate_ref.shape[0]
    tokens = pltpu.make_async_copy(token_hbm, rows_ref, sems.at[2, 0])
    tokens.start()

    def load(member, which):
        source, target = ((gate_hbm, gate_ref), (up_hbm, up_ref))[which]
        return pltpu.make_async_copy(
            source.at[member], target.at[member], sems.at[which, member]
        )

    for member in range(local_experts):
        load(member, 0).start()
        load(member, 1).start()
    tokens.wait()

    def one_expert(member, carry):
        load(member, 0).wait()
        load(member, 1).wait()
        hidden_ref[member] = hidden_of(rows_ref[...], gate_ref[member], up_ref[member])
        return carry

    lax.fori_loop(0, local_experts, one_expert, 0)


def own_hidden(tokens, w_gate, w_up):
    local_experts, _, units = w_gate.shape
    count = tokens.shape[0]
    return pl.pallas_call(
        own_kernel,
        out_shape=[
            pltpu.VMEM(w_gate.shape, w_gate.dtype),
            pltpu.VMEM(w_up.shape, w_up.dtype),
            pltpu.VMEM((local_experts, count, units), jnp.bfloat16),
        ],
        in_specs=[ANY] * 3,
        out_specs=[VMEM] * 3,
        scratch_shapes=[
            pltpu.VMEM(tokens.shape, tokens.dtype),
            pltpu.SemaphoreType.DMA((3, local_experts)),
        ],
        compiler_params=pltpu.CompilerParams(vmem_limit_bytes=8 * MIB),
        cost_estimate=pl.CostEstimate(
            flops=4 * count * w_gate.size, bytes_accessed=4 * w_gate.size, transcendentals=0
        ),
    )(in_hbm(tokens), in_hbm(w_gate), in_hbm(w_up))


def spread_shares(packed_refs, spread_ref, count, top, held):
    first = lax.axis_index("expert") * held
    slots = spread_ref.shape[1]
    expert = lax.broadcasted_iota(jnp.int32, (slots, count), 0) + first
    for index, packed_ref in enumerate(packed_refs):
        tiles = packed_ref.shape[0] - 2
        ids = packed_ref[tiles].astype(jnp.float32).astype(jnp.int32)
        shares = packed_ref[tiles + 1].astype(jnp.float32)
        spread = jnp.zeros((slots, count), jnp.float32)
        for slot in range(top):
            named = expert == ids[slot : slot + 1, :count]
            spread += jnp.where(named, shares[slot : slot + 1, :count], 0.0)
        spread_ref[index * count : (index + 1) * count, :] = spread.T


def project_into(out_refs, total_ref, spread_ref, down_ref, hidden_at, count):
    local_experts, _, width = down_ref.shape
    for member in range(local_experts):
        weight = spread_ref[:, member : member + 1]
        for start in range(0, width, CHUNK):
            span = slice(start, min(start + CHUNK, width))
            scaled = weight * jnp.dot(
                hidden_at(member), down_ref[member, :, span], preferred_element_type=jnp.float32
            )
            if member:
                scaled = total_ref[:, span] + scaled
            if member < local_experts - 1:
                total_ref[:, span] = scaled
                continue
            for index, out_ref in enumerate(out_refs):
                part = scaled[index * count : (index + 1) * count]
                out_ref[:, span] = part.astype(out_ref.dtype)


def far_kernel(blocks, sent, top, *refs):
    packed_refs = refs[:blocks]
    gate_ref, up_ref, down_hbm = refs[blocks : blocks + 3]
    outs = refs[blocks + 3 :]
    out_refs, down_ref, near_ref = outs[:sent], outs[sent], outs[sent + 1]
    rows_ref, spread_ref, hidden_ref, total_ref, sems = outs[sent + 2 :]
    local_experts, width, units = gate_ref.shape
    count = rows_ref.shape[0] // blocks
    across = width // LANES
    tiles = packed_refs[0].shape[0] - 2

    def load(member):
        return pltpu.make_async_copy(down_hbm.at[member], down_ref.at[member], sems.at[member])

    @pl.loop(0, local_experts)
    def _(member):
        load(member).start()

    for index in range(blocks):
        for tile in range(tiles):
            row = index * count + tile // across * SUBLANES
            column = tile % across * LANES
            rows_ref[row : row + SUBLANES, column : column + LANES] = packed_refs[index][tile]
    spread_shares(packed_refs[:sent], spread_ref, count, top, local_experts)
    for member in range(local_experts):
        for start in range(0, units, CHUNK):
            span = slice(start, min(start + CHUNK, units))
            hidden = hidden_of(rows_ref[...], gate_ref[member, :, span], up_ref[member, :, span])
            hidden_ref[member, :, span] = hidden[: sent * count]
            if sent < blocks:
                near_ref[member, :, span] = hidden[sent * count :]
    for member in range(local_experts):
        load(member).wait()
    project_into(
        out_refs, total_ref, spread_ref, down_ref, lambda member: hidden_ref[member], count
    )


def far(packed, sent, gate, up, w_down, count, top):
    blocks = len(packed)
    local_experts, units, width = w_down.shape
    rows = blocks * count
    near_rows = max(rows - sent * count, SUBLANES)
    *parts, down, near_hidden = pl.pallas_call(
        functools.partial(far_kernel, blocks, sent, top),
        out_shape=[jax.ShapeDtypeStruct((count, width), jnp.bfloat16)] * sent
        + [
            pltpu.VMEM(w_down.shape, w_down.dtype),
            pltpu.VMEM((local_experts, near_rows, units), jnp.bfloat16),
        ],
        in_specs=[VMEM] * (blocks + 2) + [ANY],
        out_specs=[VMEM] * (sent + 2),
        scratch_shapes=[
            pltpu.VMEM((rows, width), jnp.bfloat16),
            pltpu.VMEM((sent * count, slots_of(local_experts)), jnp.float32),
            pltpu.VMEM((local_experts, sent * count, units), jnp.bfloat16),
            pltpu.VMEM((sent * count, width), jnp.float32),
            pltpu.SemaphoreType.DMA((local_experts,)),
        ],
        compiler_params=pltpu.CompilerParams(vmem_limit_bytes=12 * MIB),
        cost_estimate=pl.CostEstimate(
            flops=6 * rows * w_down.size, bytes_accessed=2 * w_down.size, transcendentals=0
        ),
    )(*packed, gate, up, in_hbm(w_down))
    return parts, down, near_hidden


def near_kernel(blocks, top, *refs):
    packed_refs, hidden_refs = refs[:blocks], refs[blocks : blocks + 2]
    down_ref = refs[blocks + 2]
    out_refs = refs[blocks + 3 : 2 * blocks + 3]
    spread_ref, hidden_ref, total_ref = refs[2 * blocks + 3 :]
    count = hidden_refs[0].shape[1]
    spread_shares(packed_refs, spread_ref, count, top, down_ref.shape[0])
    hidden_ref[:, :count, :] = hidden_refs[0][...]
    hidden_ref[:, count:, :] = hidden_refs[1][...]
    project_into(
        out_refs, total_ref, spread_ref, down_ref, lambda member: hidden_ref[member], count
    )


def near(packed, hiddens, down, kinds, top):
    blocks = len(packed)
    local_experts, count, units = hiddens[0].shape
    width = down.shape[2]
    rows = blocks * count
    return pl.pallas_call(
        functools.partial(near_kernel, blocks, top),
        out_shape=[jax.ShapeDtypeStruct((count, width), kind) for kind in kinds],
        in_specs=[VMEM] * (blocks + 3),
        out_specs=[VMEM] * blocks,
        scratch_shapes=[
            pltpu.VMEM((rows, slots_of(local_experts)), jnp.float32),
            pltpu.VMEM((local_experts, rows, units), jnp.bfloat16),
            pltpu.VMEM((rows, width), jnp.float32),
        ],
        compiler_params=pltpu.CompilerParams(vmem_limit_bytes=10 * MIB),
        cost_estimate=pl.CostEstimate(
            flops=2 * rows * down.size, bytes_accessed=2 * down.size, transcendentals=0
        ),
    )(*packed, *hiddens, down)


def exchange(array, pairs):
    return lax.ppermute(array, "expert", pairs)


def per_device(tokens, expert_ids, route_scores, w_gate, w_up, w_down):
    peers = lax.axis_size("expert")
    count, top = expert_ids.shape
    packed = pack(tokens, expert_ids, route_scores)
    if peers == 4:
        pairs = {shift: [(i, i ^ shift) for i in range(peers)] for shift in (2, 3, 1)}
        got = {s: exchange(packed, pairs[s]) for s in pairs}
        gate, up, own = own_hidden(tokens, w_gate, w_up)
        order = [got[3], got[2], got[1]]
        parts, down, beside = far(order, 1, gate, up, w_down, count, top)
        hop = exchange(parts[0], pairs[1])
        kinds = (jnp.float32, jnp.float32, jnp.bfloat16)
        total, part, beside_part = near([packed, got[2], got[1]], [own, beside], down, kinds, top)
        both = (part + hop.astype(jnp.float32)).astype(jnp.bfloat16)
        back = [exchange(both, pairs[2]), exchange(beside_part, pairs[1])]
        for part in back:
            total = total + part.astype(jnp.float32)
        return total.astype(jnp.bfloat16)
    got = lax.all_gather(packed, "expert")
    gate, up, _ = own_hidden(tokens, w_gate, w_up)
    parts = []
    for start in range(0, peers, GROUP):
        here = [got[i] for i in range(start, min(start + GROUP, peers))]
        parts += far(here, len(here), gate, up, w_down, count, top)[0]
    back = lax.all_to_all(jnp.stack(parts), "expert", 0, 0, tiled=True)
    return jnp.sum(back.astype(jnp.float32), axis=0).astype(jnp.bfloat16)


def solution(mesh):
    split = P(("groups", "expert", "dp"), None)
    held = P("expert", None, None)
    return jax.shard_map(
        per_device,
        mesh=mesh,
        in_specs=(split, split, split, held, held, held),
        out_specs=split,
        check_vma=False,
    )
```
